32 devices in a mesh: member: 2 (over y), cell: 16 (over z, x, core).
Axes of the slice: x: 2, y: 2, z: 4, core: 2. Of those that a mesh axis runs over, the one named last changes fastest.
Arguments:
- wave_energy: float32 [2304, 2048], P(('member', 'cell')), parts along dimension 0, may hold values from -6 to 6
- courant: float32 [1152], replicated, may hold values from -0.9 to 0.9
- sea_mask: int32 [2048], replicated, may hold values 0 or 1
- lift_weight: bfloat16 [1024, 1152], replicated, may hold values from -0.1875 to 0.1875
- back_weight: bfloat16 [1152, 1024], replicated, may hold values from -0.1875 to 0.1875
Outputs:
- wave_next: float32 [2304, 2048], P(('member', 'cell')), parts along dimension 0
The draws below stay inside these ranges and needn't reach their ends.
There are 2 independent parts, one for each index of `member`. The reference program is written for one: setup_inputs(seed, part) draws one part's arguments, and reference() takes and returns one part's arrays. A program takes and returns all parts, laid end to end along the dimension named above; an argument that names none is the same for every part. Nothing has to cross between parts.
All inputs are finite; a program needn't handle non-finite values.
Results may differ from the reference program's by a relative error of at most 0.0026.
Values sent between devices are 32-bit elements; how exact they have to be, the bound alone decides.
A program may use at most 64 MiB of HBM per device.

```python
import jax
import jax.numpy as jnp
from jax import lax

K = 1152
R = 1024
CELL_DEV = 128
STEPS = 2
NC = 2048
N_CELL = 16


def place_ends(values, rng, low, high):
    longest = values.shape.index(max(values.shape))
    spots = []
    for shift in (0, 1):
        where = [jax.random.randint(jax.random.fold_in(rng, axis), (), 0, length) for axis, length in enumerate(values.shape)]
        where[longest] = (where[longest] + shift) % values.shape[longest]
        spots.append(tuple(where))
    return values.at[spots[0]].set(low).at[spots[1]].set(high)


def level_of(key, dims, split, smallest, largest):
    gain, own = 1.0, jax.random.fold_in(key, 6)
    for dim, parts in split:
        steps = jnp.exp(jax.random.uniform(jax.random.fold_in(own, dim), (parts,), jnp.float32, smallest / len(split), largest / len(split)))
        gain = gain * jnp.repeat(steps, dims[dim] // parts).reshape([-1 if axis == dim else 1 for axis in range(len(dims))])
    return gain


def bell_draw(key, dims, scale, bound, shards=(), dtype=jnp.bfloat16):
    gain = level_of(key, dims, shards, -0.22, 0.18) if shards else 1.0
    entries = jax.random.normal(key, dims, jnp.float32) * scale * gain
    return jnp.minimum(jnp.maximum(entries, -bound), bound).astype(dtype)


def setup_inputs(seed: int = 0, part: int = 0) -> dict:
    seeds = jax.random.split(jax.random.key(seed), 6)
    part_splits = jax.random.split(jax.random.fold_in(seeds[5], part), 6)
    return {
        "wave_energy": bell_draw(part_splits[0], (K, NC), 1.0, 6.0, ((0, 16),), jnp.float32),
        "courant": jnp.clip(jax.random.uniform(seeds[1], (K,), jnp.float32, -0.9, 0.9), -0.9, 0.9),
        "sea_mask": place_ends((jax.random.randint(seeds[2], (NC,), 0, 10) < 7).astype(jnp.int32), jax.random.fold_in(seeds[2], 1), 0, 1),
        "lift_weight": bell_draw(seeds[3], (R, K), K ** -0.5, 0.1875),
        "back_weight": bell_draw(seeds[4], (K, R), R ** -0.5, 0.1875),
    }


coupling = 0.25


def minmod(first_term, second_term):
    return 0.5 * (jnp.sign(first_term) + jnp.sign(second_term)) * jnp.minimum(jnp.abs(first_term), jnp.abs(second_term))


def substep(spectra, sea_field, speeds):
    extent_cells = spectra.shape[1]
    differences = spectra[:, 1:] - spectra[:, :-1]
    slopes = minmod(differences[:, 1:], differences[:, :-1])
    forward_speed = jnp.maximum(speeds, 0.0)
    backward_speed = jnp.minimum(speeds, 0.0)
    open_faces = sea_field[1:extent_cells - 2] * sea_field[2:extent_cells - 1]
    fluxes = forward_speed * (spectra[:, 1:extent_cells - 2] + 0.5 * (1.0 - forward_speed) * slopes[:, 0:extent_cells - 3])
    fluxes = fluxes + backward_speed * (spectra[:, 2:extent_cells - 1] - 0.5 * (1.0 + backward_speed) * slopes[:, 1:extent_cells - 2])
    fluxes = fluxes * open_faces
    return spectra[:, 2:extent_cells - 2] - (fluxes[:, 1:] - fluxes[:, :-1])


def reference(wave_energy, courant, sea_mask, lift_weight, back_weight):
    sea_field = sea_mask.astype(jnp.float32)
    sea_padded = jnp.pad(sea_field, 2)
    groups = K // N_CELL

    def propagate(inputs):
        block_state, speeds = inputs
        for turn_index in range(2):
            block_state = substep(jnp.pad(block_state, ((0, 0), (2, 2))), sea_padded, speeds[:, None])
        return block_state

    def fourwave(block_state):
        lifted = jnp.dot(lift_weight, block_state.astype(jnp.bfloat16), preferred_element_type=jnp.float32)
        squared = (lifted * lifted).astype(jnp.bfloat16)
        source = jnp.dot(back_weight, squared, preferred_element_type=jnp.float32)
        return block_state + coupling * source

    spectra = wave_energy
    for repeat in range(STEPS):
        spectra = lax.map(propagate, (spectra.reshape(N_CELL, groups, NC), courant.reshape(N_CELL, groups))).reshape(K, NC)
        cell_tiles = spectra.reshape(K, N_CELL, CELL_DEV).transpose(1, 0, 2)
        spectra = lax.map(fourwave, cell_tiles).transpose(1, 0, 2).reshape(K, NC)
    return spectra
```

```python
import functools

import jax
import jax.numpy as jnp
from jax import lax
from jax.experimental import pallas as pl
from jax.experimental.pallas import tpu as pltpu
from jax.sharding import PartitionSpec as P

STEPS = 2
LANES = 128
MESH = pl.DeviceIdType.MESH

coupling = 0.25


def minmod(first_term, second_term):
    low = jnp.minimum(first_term, second_term)
    high = jnp.maximum(first_term, second_term)
    return jnp.maximum(low, 0.0) + jnp.minimum(high, 0.0)


def step_pair(spectra, open_faces, speeds):
    width = spectra.shape[1]
    eastward = speeds >= 0.0
    weight = jnp.where(eastward, 0.5 * (1.0 - speeds), -0.5 * (1.0 + speeds))
    open_before = pltpu.roll(open_faces, 1, 1)
    for _ in range(2):
        ahead = pltpu.roll(spectra, width - 1, 1) - spectra
        behind = spectra - pltpu.roll(spectra, 1, 1)
        carried = speeds * (spectra + weight * minmod(ahead, behind))
        after = jnp.where(eastward, carried, pltpu.roll(carried, width - 1, 1))
        before = jnp.where(eastward, pltpu.roll(carried, 1, 1), carried)
        spectra = spectra - (after * open_faces - before * open_before)
    return spectra


def kernel(
    n, u_ref, speed_ref, sea_ref, lift_hbm, back_hbm, out_ref,
    sent, got, state, rounded, squared, result, sea, speeds, lift, back,
    load_sem, own_sem, send_one, recv_one, send_two, recv_two,
):
    me = lax.axis_index("cell")
    depth = u_ref.shape[0]
    packs = depth // 8
    modes, comps = lift.shape

    barrier = pltpu.get_barrier_semaphore()

    def greet(k, _):
        other = lax.rem(me + k, n)
        pl.semaphore_signal(barrier, inc=1, device_id={"cell": other}, device_id_type=MESH)
        return 0

    lax.fori_loop(1, n, greet, 0)
    load_lift = pltpu.make_async_copy(lift_hbm, lift, load_sem.at[0])
    load_back = pltpu.make_async_copy(back_hbm, back, load_sem.at[1])
    load_lift.start()
    load_back.start()

    cells = n * LANES
    half = n // 2
    tile_of = lambda device: device // 2 + lax.rem(device, 2) * half
    my_tile = tile_of(me)
    sea_row = sea_ref[...].astype(jnp.float32)
    sea[:, LANES : cells + LANES] = jnp.broadcast_to(sea_row, (8, cells))
    sea[:, :LANES] = jnp.zeros((8, LANES), jnp.float32)
    sea[:, cells + LANES :] = jnp.zeros((8, LANES), jnp.float32)
    lane = lax.broadcasted_iota(jnp.int32, (8, LANES), 1)

    for r in range(speed_ref.shape[0]):
        row = jnp.broadcast_to(speed_ref[r : r + 1, :], (LANES, LANES))
        speeds[r * LANES : (r + 1) * LANES, :] = jnp.transpose(row)

    def first(dest, source):
        return pltpu.make_async_remote_copy(
            src_ref=sent.at[dest], dst_ref=got.at[source],
            send_sem=send_one.at[dest], recv_sem=recv_one.at[source],
            device_id={"cell": dest}, device_id_type=MESH,
        )

    empty = jnp.zeros((8, LANES), jnp.float32)
    for phase in range(2):
        low = phase * half
        near = sea[:, low * LANES : (low + half + 2) * LANES]
        faces = near * pltpu.roll(near, (half + 2) * LANES - 1, 1)
        for g in range(packs):
            rows = pl.ds(g * 8, 8)
            own_rows = pl.ds(pl.multiple_of(me * depth + g * 8, 8), 8)
            if phase:
                parts = [u_ref[rows, (low - 1) * LANES :], empty]
            else:
                parts = [empty, u_ref[rows, : (half + 1) * LANES]]
            block = jnp.concatenate(parts, axis=1)
            own_speeds = jnp.concatenate([speeds[own_rows, :]] * (half + 2), axis=1)
            block = step_pair(block, faces, own_speeds)
            tiles = [block[:, t * LANES : (t + 1) * LANES] for t in range(half + 2)]
            for t in range(half):
                dest = 2 * t + phase
                sent[dest, rows, :] = tiles[t + 1]
                edge = jnp.where(lane < 64, tiles[t + 2], tiles[t])
                if g:
                    edge = pltpu.roll(edge, 8 * g, 1)
                    mine = (lane >= 8 * g - 4) & (lane < 8 * g + 4)
                    edge = jnp.where(mine, edge, sent[dest, depth : depth + 8, :])
                sent[dest, depth : depth + 8, :] = edge
        if not phase:
            pl.semaphore_wait(barrier, n - 1)

        def push(k, _):
            dest = 2 * lax.rem(me // 2 + half - k, half) + phase

            @pl.when(dest != me)
            def _():
                first(dest, me).start()

            return 0

        lax.fori_loop(0, half, push, 0)

    last_sea, main_sea, next_sea = [
        sea[:, pl.ds(pl.multiple_of((my_tile + k) * LANES, LANES), LANES)] for k in range(3)
    ]
    side_sea = jnp.where(lane < 4, next_sea, jnp.where(lane >= LANES - 4, last_sea, 0.0))
    near_sea = jnp.concatenate([main_sea, side_sea], axis=1)
    near_open = (near_sea * pltpu.roll(near_sea, 2 * LANES - 1, 1))[0:1, :]

    def unpack(source, block):
        halo = (lane < 4) | (lane >= LANES - 4)
        edge = block[depth : depth + 8, :]
        for g in range(packs):
            rows = pl.ds(pl.multiple_of(source * depth + g * 8, 8), 8)
            state[rows, 0:LANES] = block[g * 8 : g * 8 + 8, :]
            turned = pltpu.roll(edge, LANES - 8 * g, 1) if g else edge
            state[rows, LANES:] = jnp.where(halo, turned, 0.0)

    unpack(me, sent[me])

    def pull(k, _):
        source = lax.rem(me + k, n)
        first(source, source).wait_recv()
        unpack(source, got[source])
        return 0

    lax.fori_loop(1, n, pull, 0)

    wide = 64

    def narrow(i, _):
        rows = pl.ds(pl.multiple_of(i * wide, wide), wide)
        rounded[rows, :] = state[rows, :].astype(jnp.bfloat16)
        return 0

    lax.fori_loop(0, comps // wide, narrow, 0)

    mode_part, comp_part = modes // 2, comps // 4

    def lifting(width):
        def body(i, _):
            rows = pl.ds(pl.multiple_of(i * mode_part, mode_part), mode_part)
            lifted = jnp.dot(
                lift[rows, :], rounded[:, :width], preferred_element_type=jnp.float32
            )
            squared[rows, :width] = (lifted * lifted).astype(jnp.bfloat16)
            return 0

        lax.fori_loop(0, 2, body, 0)

    load_lift.wait()
    lifting(2 * LANES)
    load_back.wait()

    def source_one(i, _):
        rows = pl.ds(pl.multiple_of(i * comp_part, comp_part), comp_part)
        source = jnp.dot(back[rows, :], squared[...], preferred_element_type=jnp.float32)
        state[rows, :] = state[rows, :] + coupling * source
        return 0

    lax.fori_loop(0, 4, source_one, 0)

    slab, piece = 128, 32
    near_open = jnp.broadcast_to(near_open, (piece, 2 * LANES))

    def propagate(i, _):
        spans = [
            pl.ds(pl.multiple_of(i * slab + j * piece, piece), piece) for j in range(slab // piece)
        ]
        before = [state[rows, :] for rows in spans]
        after = [
            step_pair(block, near_open, jnp.concatenate([speeds[rows, :]] * 2, axis=1))
            for rows, block in zip(spans, before)
        ]
        for rows, block in zip(spans, after):
            state[rows, 0:LANES] = block[:, :LANES]
            rounded[rows, 0:LANES] = block[:, :LANES].astype(jnp.bfloat16)
        return 0

    lax.fori_loop(0, comps // slab, propagate, 0)
    lifting(LANES)

    def place(source):
        return out_ref.at[tile_of(source)]

    def second(dest, source):
        return pltpu.make_async_remote_copy(
            src_ref=result.at[dest], dst_ref=place(source),
            send_sem=send_two.at[dest], recv_sem=recv_two.at[source],
            device_id={"cell": dest}, device_id_type=MESH,
        )

    own = pltpu.make_async_copy(result.at[me], place(me), own_sem)
    part = n // 4

    def source_two(step, _):
        i = lax.rem(me // part + 1 + step, 4)
        rows = pl.ds(pl.multiple_of(i * comp_part, comp_part), comp_part)
        source = jnp.dot(
            back[rows, :], squared[:, :LANES], preferred_element_type=jnp.float32
        )
        total = state[rows, 0:LANES] + coupling * source
        result[pl.ds(i * part, part)] = total.reshape(part, depth, LANES)

        def send(j, _):
            dest = i * part + j

            @pl.when(dest != me)
            def _():
                second(dest, me).start()

            return 0

        lax.fori_loop(0, part, send, 0)
        return 0

    lax.fori_loop(0, 4, source_two, 0)
    own.start()

    def finish(k, _):
        dest = lax.rem(me + k, n)
        source = lax.rem(me + n - k, n)
        first(dest, me).wait_send()
        second(dest, me).wait_send()
        second(source, source).wait_recv()
        return 0

    lax.fori_loop(1, n, finish, 0)
    own.wait()


def shards(wave_energy, courant, sea_mask, lift_weight, back_weight):
    n = lax.axis_size("cell")
    groups, cells = wave_energy.shape
    modes = lift_weight.shape[0]
    depth = -(-groups // 8) * 8
    extra = depth - groups
    if extra:
        wave_energy = jnp.pad(wave_energy, ((0, extra), (0, 0)))
        courant = jnp.pad(courant.reshape(n, groups), ((0, 0), (0, extra))).reshape(-1)
        lift_weight = jnp.pad(
            lift_weight.reshape(modes, n, groups), ((0, 0), (0, 0), (0, extra))
        ).reshape(modes, n * depth)
        back_weight = jnp.pad(
            back_weight.reshape(n, groups, modes), ((0, 0), (0, extra), (0, 0))
        ).reshape(n * depth, modes)
    comps = n * depth
    speed_rows = jnp.pad(courant, (0, -comps % LANES)).reshape(-1, LANES)
    vmem = pl.BlockSpec(memory_space=pltpu.VMEM)
    anywhere = pl.BlockSpec(memory_space=pl.ANY)
    out = pl.pallas_call(
        functools.partial(kernel, n),
        out_shape=jax.ShapeDtypeStruct((n, depth, cells // n), jnp.float32),
        in_specs=[vmem, vmem, vmem, anywhere, anywhere],
        out_specs=anywhere,
        scratch_shapes=[
            pltpu.VMEM((n, depth + 8, LANES), jnp.float32),
            pltpu.VMEM((n, depth + 8, LANES), jnp.float32),
            pltpu.VMEM((comps, 2 * LANES), jnp.float32),
            pltpu.VMEM((comps, 2 * LANES), jnp.bfloat16),
            pltpu.VMEM((modes, 2 * LANES), jnp.bfloat16),
            pltpu.VMEM((n, depth, LANES), jnp.float32),
            pltpu.VMEM((8, cells + 2 * LANES), jnp.float32),
            pltpu.VMEM((speed_rows.size, LANES), jnp.float32),
            pltpu.VMEM((modes, comps), jnp.bfloat16),
            pltpu.VMEM((comps, modes), jnp.bfloat16),
            pltpu.SemaphoreType.DMA((2,)),
            pltpu.SemaphoreType.DMA,
            pltpu.SemaphoreType.DMA((n,)),
            pltpu.SemaphoreType.DMA((n,)),
            pltpu.SemaphoreType.DMA((n,)),
            pltpu.SemaphoreType.DMA((n,)),
        ],
        compiler_params=pltpu.CompilerParams(collective_id=0, has_side_effects=True),
    )(wave_energy, speed_rows, sea_mask[None, :], lift_weight, back_weight)
    return out.transpose(1, 0, 2).reshape(depth, cells)[:groups]


def solution(mesh):
    placed = (P(("member", "cell"), None), P(), P(), P(), P())
    return jax.shard_map(
        shards, mesh=mesh, in_specs=placed, out_specs=P(("member", "cell"), None), check_vma=False
    )
```

```python
import functools

import jax
import jax.numpy as jnp
from jax import lax
from jax.experimental import pallas as pl
from jax.experimental.pallas import tpu as pltpu
from jax.sharding import PartitionSpec as P

LANES = 128
EDGE = 8
GROUP = 4
MESH = pl.DeviceIdType.MESH

coupling = 0.25


def minmod(first_term, second_term):
    low = jnp.minimum(first_term, second_term)
    high = jnp.maximum(first_term, second_term)
    return jnp.maximum(low, 0.0) + jnp.minimum(high, 0.0)


def step_pair(spectra, open_faces, speeds):
    height = spectra.shape[0]
    eastward = speeds >= 0.0
    weight = jnp.where(eastward, 0.5 * (1.0 - speeds), -0.5 * (1.0 + speeds))
    eastward = jnp.broadcast_to(eastward, spectra.shape)
    for _ in range(2):
        ahead = pltpu.roll(spectra, height - 1, 0) - spectra
        behind = pltpu.roll(ahead, 1, 0)
        carried = speeds * (spectra + weight * minmod(ahead, behind))
        flux = jnp.where(eastward, carried, pltpu.roll(carried, height - 1, 0)) * open_faces
        spectra = spectra - (flux - pltpu.roll(flux, 1, 0))
    return spectra


def faces_of(sea):
    return sea * pltpu.roll(sea, sea.shape[0] - 1, 0)


def dot_rows(a, b):
    return lax.dot_general(a, b, (((1,), (1,)), ((), ())), preferred_element_type=jnp.float32)


def kernel(
    n, u_hbm, speed_hbm, sea_hbm, lift_hbm, back_hbm, out_ref,
    u, speed, sea_row, sent, got, cells_u, cells_sea, state, rounded, squared, total, result, lift, back,
    load_sem, own_sem, send_one, recv_one, send_two, recv_two,
):
    me = lax.axis_index("cell")
    depth, cells = u_hbm.shape
    modes, comps = lift.shape
    strips = comps // LANES

    half = n // 2
    spread = half // GROUP

    def owner_of(tile):
        k = lax.rem(tile, half)
        j, c = lax.rem(k, GROUP), k // GROUP
        return 2 * (j * spread + lax.rem(c + j, spread)) + tile // half

    def tile_of(device):
        chip = device // 2
        j = chip // spread
        c = lax.rem(lax.rem(chip, spread) + GROUP * spread - j, spread)
        return c * GROUP + j + lax.rem(device, 2) * half

    my_tile = tile_of(me)

    head = (GROUP + 1) * LANES
    load_sea = pltpu.make_async_copy(sea_hbm, sea_row, load_sem.at[0])
    load_speed = pltpu.make_async_copy(speed_hbm, speed, load_sem.at[1])
    load_head = pltpu.make_async_copy(u_hbm.at[:, :head], u.at[:, :head], load_sem.at[2])
    load_rest = pltpu.make_async_copy(u_hbm.at[:, head:], u.at[:, head:cells], load_sem.at[3])
    load_lift = pltpu.make_async_copy(lift_hbm, lift, load_sem.at[4])
    load_back = pltpu.make_async_copy(back_hbm, back, load_sem.at[5])
    loads = [load_sea, load_head, load_speed, load_rest, load_lift, load_back]
    for load in loads:
        load.start()

    barrier = pltpu.get_barrier_semaphore()

    def greet(k, _):
        other = lax.rem(me + k, n)
        pl.semaphore_signal(barrier, inc=1, device_id={"cell": other}, device_id_type=MESH)
        return 0

    lax.fori_loop(1, n, greet, 0)

    lane = lax.broadcasted_iota(jnp.int32, (EDGE, LANES), 1)
    after = lax.broadcasted_iota(jnp.int32, (EDGE, LANES), 0) < EDGE // 2

    none = jnp.zeros((EDGE, LANES), jnp.float32)
    cells_sea[0:EDGE, :] = none
    cells_sea[cells + EDGE :, :] = none
    cells_u[0:EDGE, :] = none
    u[:, cells:] = jnp.zeros((depth, LANES), jnp.float32)

    load_sea.wait()

    def turn_sea(c, _):
        for j in range(GROUP):
            start = pl.multiple_of((c * GROUP + j) * LANES, LANES)
            row = sea_row[:, pl.ds(start, LANES)].astype(jnp.float32)
            cells_sea[pl.ds(start + EDGE, LANES), :] = jnp.transpose(
                jnp.broadcast_to(row, (LANES, LANES))
            )
        return 0

    lax.fori_loop(0, n // GROUP, turn_sea, 0)
    load_speed.wait()

    place = me * depth
    shift = lax.rem(place, LANES)
    row = place // LANES
    row_after = jnp.minimum(row + 1, strips - 1)
    own_speeds = jnp.where(
        lane < LANES - shift,
        pltpu.roll(jnp.broadcast_to(speed[pl.ds(row, 1), :], (EDGE, LANES)), lax.rem(LANES - shift, LANES), 1),
        pltpu.roll(jnp.broadcast_to(speed[pl.ds(row_after, 1), :], (EDGE, LANES)), lax.rem(LANES - shift, LANES), 1),
    )[0:1, :]

    def turn_tile(tile):
        start = pl.multiple_of(tile * LANES, LANES)
        block = u[:, pl.ds(start, LANES)]
        if depth < LANES:
            block = jnp.concatenate([block, jnp.zeros((LANES - depth, LANES), jnp.float32)], axis=0)
        cells_u[pl.ds(start + EDGE, LANES), :] = jnp.transpose(block)

    def make_group(c):
        for j in range(1, GROUP + 1):
            turn_tile(c * GROUP + j)
        for j in range(GROUP):
            tile = c * GROUP + j
            span = pl.ds(pl.multiple_of(tile * LANES, LANES), LANES + 2 * EDGE)
            block = step_pair(cells_u[span, :], faces_of(cells_sea[span, :]), own_speeds)
            sent[tile, 0:depth, :] = jnp.transpose(block[EDGE : EDGE + LANES, :])[0:depth, :]
            edge = jnp.where(after, block[EDGE + LANES :, :], block[:EDGE, :])
            sent[tile, depth:, :] = pltpu.roll(edge, shift, 1)

    def first(tile, dest, source):
        return pltpu.make_async_remote_copy(
            src_ref=sent.at[tile], dst_ref=got.at[source],
            send_sem=send_one.at[tile], recv_sem=recv_one.at[source],
            device_id={"cell": dest}, device_id_type=MESH,
        )

    def send_group(c):
        for j in range(GROUP):
            tile = c * GROUP + j
            dest = owner_of(tile)

            @pl.when(dest != me)
            def _():
                first(tile, dest, me).start()

    load_head.wait()
    turn_tile(0)
    make_group(0)
    pl.semaphore_wait(barrier, n - 1)
    send_group(0)
    load_rest.wait()

    def next_group(c, _):
        make_group(c)
        send_group(c)
        return 0

    lax.fori_loop(1, n // GROUP, next_group, 0)

    got[me] = sent[my_tile]
    start = pl.multiple_of(my_tile * LANES, LANES)
    near_sea = [
        cells_sea[pl.ds(start + EDGE, LANES), :],
        jnp.where(after, cells_sea[pl.ds(start + EDGE + LANES, EDGE), :], cells_sea[pl.ds(start, EDGE), :]),
    ]
    near_open = faces_of(jnp.concatenate(near_sea, axis=0))

    def pull(k, _):
        source = lax.rem(me + k, n)
        first(0, source, source).wait_recv()
        return 0

    lax.fori_loop(1, n, pull, 0)

    height = LANES + EDGE
    for q in range(strips):
        low, high = q * LANES, (q + 1) * LANES
        pieces, edge = [], None
        for source in range(low // depth, -(-high // depth)):
            base = source * depth
            pieces.append(got[source, max(low - base, 0) : min(high - base, depth), :])
            mine = got[source, depth:, :]
            edge = mine if edge is None else jnp.where(lane >= base - low, mine, edge)
        block = jnp.concatenate([jnp.transpose(jnp.concatenate(pieces, axis=0)), edge], axis=0)
        state[q] = block
        rounded[:, low:high] = jnp.concatenate([block, none], axis=0).astype(jnp.bfloat16)

    load_lift.wait()
    lifted = dot_rows(rounded[...], lift[...])
    squared[...] = (lifted * lifted).astype(jnp.bfloat16)
    load_back.wait()

    parts = max(k for k in (4, 3, 2, 1) if strips % k == 0)
    wide = strips // parts
    for part in range(parts):
        rows = slice(part * wide * LANES, (part + 1) * wide * LANES)
        source = dot_rows(squared[...], back[rows, :])
        for k in range(wide):
            q = part * wide + k
            block = state[q] + coupling * source[:height, k * LANES : (k + 1) * LANES]
            block = step_pair(block, near_open, speed[q : q + 1, :])[:LANES, :]
            rounded[:LANES, q * LANES : (q + 1) * LANES] = block.astype(jnp.bfloat16)
            total[q * LANES : (q + 1) * LANES, :] = jnp.transpose(block)

    lifted = dot_rows(rounded[:LANES, :], lift[...])
    squared[:LANES, :] = (lifted * lifted).astype(jnp.bfloat16)

    def column(tile):
        return out_ref.at[:, pl.ds(pl.multiple_of(tile * LANES, LANES), LANES)]

    def second(dest, source):
        return pltpu.make_async_remote_copy(
            src_ref=result.at[dest], dst_ref=column(tile_of(source)),
            send_sem=send_two.at[dest], recv_sem=recv_two.at[source],
            device_id={"cell": dest}, device_id_type=MESH,
        )

    own = pltpu.make_async_copy(result.at[me], column(my_tile), own_sem)
    part = n // 4
    comp_part = comps // 4

    def source_two(step, _):
        i = lax.rem(me // part + 1 + step, 4)
        rows = pl.ds(pl.multiple_of(i * comp_part, comp_part), comp_part)
        source = dot_rows(back[rows, :], squared[:LANES, :])
        ended = total[rows, :] + coupling * source
        result[pl.ds(i * part, part)] = ended.reshape(part, depth, LANES)

        def send(j, _):
            dest = i * part + j

            @pl.when(dest != me)
            def _():
                second(dest, me).start()

            return 0

        lax.fori_loop(0, part, send, 0)
        return 0

    lax.fori_loop(0, 4, source_two, 0)
    own.start()

    def finish(k, _):
        dest = lax.rem(me + k, n)
        source = lax.rem(me + n - k, n)
        first(tile_of(dest), dest, me).wait_send()
        second(dest, me).wait_send()
        second(source, source).wait_recv()
        return 0

    lax.fori_loop(1, n, finish, 0)
    own.wait()


def shards(wave_energy, courant, sea_mask, lift_weight, back_weight):
    n = lax.axis_size("cell")
    groups, cells = wave_energy.shape
    modes = lift_weight.shape[0]
    depth = -(-groups // 8) * 8
    extra = depth - groups
    if extra:
        wave_energy = jnp.pad(wave_energy, ((0, extra), (0, 0)))
        courant = jnp.pad(courant.reshape(n, groups), ((0, 0), (0, extra))).reshape(-1)
        lift_weight = jnp.pad(
            lift_weight.reshape(modes, n, groups), ((0, 0), (0, 0), (0, extra))
        ).reshape(modes, n * depth)
        back_weight = jnp.pad(
            back_weight.reshape(n, groups, modes), ((0, 0), (0, extra), (0, 0))
        ).reshape(n * depth, modes)
    comps = n * depth
    strips = comps // LANES
    tall = LANES + 2 * EDGE
    anywhere = pl.BlockSpec(memory_space=pl.ANY)
    out = pl.pallas_call(
        functools.partial(kernel, n),
        out_shape=jax.ShapeDtypeStruct((depth, cells), jnp.float32),
        in_specs=[anywhere] * 5,
        out_specs=anywhere,
        scratch_shapes=[
            pltpu.VMEM((depth, cells + LANES), jnp.float32),
            pltpu.VMEM((strips, LANES), jnp.float32),
            pltpu.VMEM((1, cells), jnp.int32),
            pltpu.VMEM((n, depth + EDGE, LANES), jnp.float32),
            pltpu.VMEM((n, depth + EDGE, LANES), jnp.float32),
            pltpu.VMEM((cells + LANES + EDGE, LANES), jnp.float32),
            pltpu.VMEM((cells + 2 * EDGE, LANES), jnp.float32),
            pltpu.VMEM((strips, LANES + EDGE, LANES), jnp.float32),
            pltpu.VMEM((tall, comps), jnp.bfloat16),
            pltpu.VMEM((tall, modes), jnp.bfloat16),
            pltpu.VMEM((comps, LANES), jnp.float32),
            pltpu.VMEM((n, depth, LANES), jnp.float32),
            pltpu.VMEM((modes, comps), jnp.bfloat16),
            pltpu.VMEM((comps, modes), jnp.bfloat16),
            pltpu.SemaphoreType.DMA((6,)),
            pltpu.SemaphoreType.DMA,
            pltpu.SemaphoreType.DMA((n,)),
            pltpu.SemaphoreType.DMA((n,)),
            pltpu.SemaphoreType.DMA((n,)),
            pltpu.SemaphoreType.DMA((n,)),
        ],
        compiler_params=pltpu.CompilerParams(
            collective_id=0, has_side_effects=True, vmem_limit_bytes=56 * 1024 * 1024
        ),
    )(wave_energy, courant.reshape(strips, LANES), sea_mask[None, :], lift_weight, back_weight)
    return out[:groups]


def solution(mesh):
    placed = (P(("member", "cell"), None), P(), P(), P(), P())
    return jax.shard_map(
        shards, mesh=mesh, in_specs=placed, out_specs=P(("member", "cell"), None), check_vma=False
    )
```

```python
import functools
import math

import jax
import jax.numpy as jnp
from jax import lax
from jax.experimental import pallas as pl
from jax.experimental.pallas import tpu as pltpu
from jax.sharding import PartitionSpec as P

LANES = 128
EDGE = 8
GROUP = 4
MESH = pl.DeviceIdType.MESH

coupling = 0.25


def minmod(first_term, second_term):
    low = jnp.minimum(first_term, second_term)
    high = jnp.maximum(first_term, second_term)
    return jnp.maximum(low, 0.0) + jnp.minimum(high, 0.0)


def step_pair(spectra, open_faces, speeds):
    height = spectra.shape[0]
    eastward = speeds >= 0.0
    weight = jnp.where(eastward, 0.5 * (1.0 - speeds), -0.5 * (1.0 + speeds))
    eastward = jnp.broadcast_to(eastward, spectra.shape)
    for _ in range(2):
        ahead = pltpu.roll(spectra, height - 1, 0) - spectra
        behind = pltpu.roll(ahead, 1, 0)
        carried = speeds * (spectra + weight * minmod(ahead, behind))
        flux = jnp.where(eastward, carried, pltpu.roll(carried, height - 1, 0)) * open_faces
        spectra = spectra - (flux - pltpu.roll(flux, 1, 0))
    return spectra


def faces_of(sea):
    return sea * pltpu.roll(sea, sea.shape[0] - 1, 0)


def dot_rows(a, b):
    return lax.dot_general(a, b, (((1,), (1,)), ((), ())), preferred_element_type=jnp.float32)


def kernel(
    n, u_hbm, speed_hbm, sea_hbm, lift_hbm, back_hbm, out_ref,
    u, speed, sea_row, sent, got, cells_u, cells_sea, state, rounded, squared, total, result, lift, back,
    load_sem, own_sem, send_one, recv_one, send_two, recv_two,
):
    me = lax.axis_index("cell")
    depth, cells = u_hbm.shape
    modes, comps = lift.shape
    strips = comps // LANES
    half = n // 2

    barrier = pltpu.get_barrier_semaphore()

    def greet(k, _):
        other = lax.rem(me + k + half, n)

        @pl.when(other != me)
        def _():
            pl.semaphore_signal(barrier, inc=1, device_id={"cell": other}, device_id_type=MESH)

        return 0

    lax.fori_loop(0, n, greet, 0)

    spread = half // GROUP

    def owner_of(tile):
        k = lax.rem(tile, half)
        j, c = lax.rem(k, GROUP), k // GROUP
        return 2 * (j * spread + lax.rem(c + j, spread)) + tile // half

    def tile_of(device):
        chip = device // 2
        j = chip // spread
        c = lax.rem(lax.rem(chip, spread) + GROUP * spread - j, spread)
        return c * GROUP + j + lax.rem(device, 2) * half

    my_tile = tile_of(me)

    head = (GROUP + 1) * LANES
    load_sea = pltpu.make_async_copy(sea_hbm, sea_row, load_sem.at[0])
    load_speed = pltpu.make_async_copy(speed_hbm, speed, load_sem.at[1])
    load_head = pltpu.make_async_copy(u_hbm.at[:, :head], u.at[:, :head], load_sem.at[2])
    load_rest = pltpu.make_async_copy(u_hbm.at[:, head:], u.at[:, head:cells], load_sem.at[3])
    load_lift = pltpu.make_async_copy(lift_hbm, lift, load_sem.at[4])
    load_back = pltpu.make_async_copy(back_hbm, back, load_sem.at[5])
    loads = [load_sea, load_head, load_speed, load_rest, load_lift, load_back]
    for load in loads:
        load.start()

    lane = lax.broadcasted_iota(jnp.int32, (EDGE, LANES), 1)
    after = lax.broadcasted_iota(jnp.int32, (EDGE, LANES), 0) < EDGE // 2

    none = jnp.zeros((EDGE, LANES), jnp.float32)
    cells_sea[0:EDGE, :] = none
    cells_sea[cells + EDGE :, :] = none
    cells_u[0:EDGE, :] = none
    u[:, cells:] = jnp.zeros((depth, LANES), jnp.float32)

    load_sea.wait()

    def turn_sea(c, _):
        for j in range(GROUP):
            start = pl.multiple_of((c * GROUP + j) * LANES, LANES)
            row = sea_row[:, pl.ds(start, LANES)].astype(jnp.float32)
            cells_sea[pl.ds(start + EDGE, LANES), :] = jnp.transpose(
                jnp.broadcast_to(row, (LANES, LANES))
            )
        return 0

    lax.fori_loop(0, n // GROUP, turn_sea, 0)
    load_speed.wait()

    place = me * depth
    shift = lax.rem(place, LANES)
    row = place // LANES
    row_after = jnp.minimum(row + 1, strips - 1)
    own_speeds = jnp.where(
        lane < LANES - shift,
        pltpu.roll(jnp.broadcast_to(speed[pl.ds(row, 1), :], (EDGE, LANES)), lax.rem(LANES - shift, LANES), 1),
        pltpu.roll(jnp.broadcast_to(speed[pl.ds(row_after, 1), :], (EDGE, LANES)), lax.rem(LANES - shift, LANES), 1),
    )[0:1, :]

    def turn_tile(tile):
        start = pl.multiple_of(tile * LANES, LANES)
        block = u[:, pl.ds(start, LANES)]
        if depth < LANES:
            block = jnp.concatenate([block, jnp.zeros((LANES - depth, LANES), jnp.float32)], axis=0)
        cells_u[pl.ds(start + EDGE, LANES), :] = jnp.transpose(block)

    def make_group(c):
        for j in range(1, GROUP + 1):
            turn_tile(c * GROUP + j)
        for j in range(GROUP):
            tile = c * GROUP + j
            span = pl.ds(pl.multiple_of(tile * LANES, LANES), LANES + 2 * EDGE)
            block = step_pair(cells_u[span, :], faces_of(cells_sea[span, :]), own_speeds)
            sent[tile, 0:depth, :] = jnp.transpose(block[EDGE : EDGE + LANES, :])[0:depth, :]
            edge = jnp.where(after, block[EDGE + LANES :, :], block[:EDGE, :])
            sent[tile, depth:, :] = pltpu.roll(edge, shift, 1)

    def first(tile, dest, source):
        return pltpu.make_async_remote_copy(
            src_ref=sent.at[tile], dst_ref=got.at[source],
            send_sem=send_one.at[tile], recv_sem=recv_one.at[source],
            device_id={"cell": dest}, device_id_type=MESH,
        )

    def send_group(c):
        for j in range(GROUP):
            tile = c * GROUP + j
            dest = owner_of(tile)

            @pl.when(dest != me)
            def _():
                first(tile, dest, me).start()

    load_head.wait()
    turn_tile(0)
    make_group(0)
    pl.semaphore_wait(barrier, n - 1)
    send_group(0)
    load_rest.wait()

    def next_group(c, _):
        make_group(c)
        send_group(c)
        return 0

    lax.fori_loop(1, n // GROUP, next_group, 0)

    got[me] = sent[my_tile]
    start = pl.multiple_of(my_tile * LANES, LANES)
    near_sea = [
        cells_sea[pl.ds(start + EDGE, LANES), :],
        jnp.where(after, cells_sea[pl.ds(start + EDGE + LANES, EDGE), :], cells_sea[pl.ds(start, EDGE), :]),
    ]
    near_open = faces_of(jnp.concatenate(near_sea, axis=0))

    def pull(k, _):
        source = lax.rem(me + k, n)
        first(0, source, source).wait_recv()
        return 0

    lax.fori_loop(1, n, pull, 0)

    height = LANES + EDGE
    for q in range(strips):
        low, high = q * LANES, (q + 1) * LANES
        pieces, edge = [], None
        for source in range(low // depth, -(-high // depth)):
            base = source * depth
            pieces.append(got[source, max(low - base, 0) : min(high - base, depth), :])
            mine = got[source, depth:, :]
            edge = mine if edge is None else jnp.where(lane >= base - low, mine, edge)
        block = jnp.concatenate([jnp.transpose(jnp.concatenate(pieces, axis=0)), edge], axis=0)
        state[q] = block
        rounded[:, low:high] = jnp.concatenate([block, none], axis=0).astype(jnp.bfloat16)

    load_lift.wait()
    lifted = dot_rows(rounded[...], lift[...])
    squared[...] = (lifted * lifted).astype(jnp.bfloat16)
    load_back.wait()

    parts = max(k for k in (4, 3, 2, 1) if strips % k == 0)
    wide = strips // parts
    for part in range(parts):
        rows = slice(part * wide * LANES, (part + 1) * wide * LANES)
        source = dot_rows(squared[...], back[rows, :])
        for k in range(wide):
            q = part * wide + k
            block = state[q] + coupling * source[:height, k * LANES : (k + 1) * LANES]
            block = step_pair(block, near_open, speed[q : q + 1, :])[:LANES, :]
            rounded[:LANES, q * LANES : (q + 1) * LANES] = block.astype(jnp.bfloat16)
            total[q * LANES : (q + 1) * LANES, :] = jnp.transpose(block)

    lifted = dot_rows(rounded[:LANES, :], lift[...])
    squared[:LANES, :] = (lifted * lifted).astype(jnp.bfloat16)

    def column(tile):
        return out_ref.at[:, pl.ds(pl.multiple_of(tile * LANES, LANES), LANES)]

    def second(dest, source):
        return pltpu.make_async_remote_copy(
            src_ref=result.at[dest], dst_ref=column(tile_of(source)),
            send_sem=send_two.at[dest], recv_sem=recv_two.at[source],
            device_id={"cell": dest}, device_id_type=MESH,
        )

    own = pltpu.make_async_copy(result.at[me], column(my_tile), own_sem)
    part = n // 4
    comp_part = comps // 4

    def source_two(step, _):
        i = lax.rem(me // part + 1 + step, 4)
        rows = pl.ds(pl.multiple_of(i * comp_part, comp_part), comp_part)
        source = dot_rows(back[rows, :], squared[:LANES, :])
        ended = total[rows, :] + coupling * source
        result[pl.ds(i * part, part)] = ended.reshape(part, depth, LANES)

        def send(j, _):
            dest = i * part + j

            @pl.when(dest != me)
            def _():
                second(dest, me).start()

            return 0

        lax.fori_loop(0, part, send, 0)
        return 0

    lax.fori_loop(0, 4, source_two, 0)
    own.start()

    def finish(k, _):
        dest = lax.rem(me + k, n)
        source = lax.rem(me + n - k, n)
        first(tile_of(dest), dest, me).wait_send()
        second(dest, me).wait_send()
        second(source, source).wait_recv()
        return 0

    lax.fori_loop(1, n, finish, 0)
    own.wait()


def shards(wave_energy, courant, sea_mask, lift_weight, back_weight):
    n = lax.axis_size("cell")
    groups, cells = wave_energy.shape
    modes = lift_weight.shape[0]
    depth = -(-groups // 8) * 8
    extra = depth - groups
    if extra:
        wave_energy = jnp.pad(wave_energy, ((0, extra), (0, 0)))
        courant = jnp.pad(courant.reshape(n, groups), ((0, 0), (0, extra))).reshape(-1)
        lift_weight = jnp.pad(
            lift_weight.reshape(modes, n, groups), ((0, 0), (0, 0), (0, extra))
        ).reshape(modes, n * depth)
        back_weight = jnp.pad(
            back_weight.reshape(n, groups, modes), ((0, 0), (0, extra), (0, 0))
        ).reshape(n * depth, modes)
    comps = n * depth
    strips = comps // LANES
    tall = LANES + 2 * EDGE
    buffers = [
        pltpu.VMEM((depth, cells + LANES), jnp.float32),
        pltpu.VMEM((strips, LANES), jnp.float32),
        pltpu.VMEM((1, cells), jnp.int32),
        pltpu.VMEM((n, depth + EDGE, LANES), jnp.float32),
        pltpu.VMEM((n, depth + EDGE, LANES), jnp.float32),
        pltpu.VMEM((cells + LANES + EDGE, LANES), jnp.float32),
        pltpu.VMEM((cells + 2 * EDGE, LANES), jnp.float32),
        pltpu.VMEM((strips, LANES + EDGE, LANES), jnp.float32),
        pltpu.VMEM((tall, comps), jnp.bfloat16),
        pltpu.VMEM((tall, modes), jnp.bfloat16),
        pltpu.VMEM((comps, LANES), jnp.float32),
        pltpu.VMEM((n, depth, LANES), jnp.float32),
        pltpu.VMEM((modes, comps), jnp.bfloat16),
        pltpu.VMEM((comps, modes), jnp.bfloat16),
    ]
    held = sum(math.prod(b.shape) * jnp.dtype(b.dtype).itemsize for b in buffers)
    operands = [
        pltpu.with_memory_space_constraint(x, pltpu.HBM)
        for x in (wave_energy, courant.reshape(strips, LANES), sea_mask[None, :], lift_weight, back_weight)
    ]
    out = pl.pallas_call(
        functools.partial(kernel, n),
        out_shape=jax.ShapeDtypeStruct((depth, cells), jnp.float32),
        in_specs=[pl.BlockSpec(memory_space=pltpu.HBM)] * 5,
        out_specs=pl.BlockSpec(memory_space=pl.ANY),
        scratch_shapes=buffers
        + [
            pltpu.SemaphoreType.DMA((6,)),
            pltpu.SemaphoreType.DMA,
            pltpu.SemaphoreType.DMA((n,)),
            pltpu.SemaphoreType.DMA((n,)),
            pltpu.SemaphoreType.DMA((n,)),
            pltpu.SemaphoreType.DMA((n,)),
        ],
        compiler_params=pltpu.CompilerParams(
            collective_id=0, has_side_effects=True, vmem_limit_bytes=held + 4 * 1024 * 1024
        ),
    )(*operands)
    return out[:groups]


def solution(mesh):
    placed = (P(("member", "cell"), None), P(), P(), P(), P())
    return jax.shard_map(
        shards, mesh=mesh, in_specs=placed, out_specs=P(("member", "cell"), None), check_vma=False
    )
```

```python
import functools
import math

import jax
import jax.numpy as jnp
from jax import lax
from jax.experimental import pallas as pl
from jax.experimental.pallas import tpu as pltpu
from jax.sharding import PartitionSpec as P

LANES = 128
EDGE = 8
GROUP = 4
MESH = pl.DeviceIdType.MESH

coupling = 0.25


def minmod(first_term, second_term):
    low = jnp.minimum(first_term, second_term)
    high = jnp.maximum(first_term, second_term)
    return jnp.maximum(low, 0.0) + jnp.minimum(high, 0.0)


def step_pair(spectra, open_faces, speeds):
    height = spectra.shape[0]
    eastward = speeds >= 0.0
    weight = jnp.where(eastward, 0.5 * (1.0 - speeds), -0.5 * (1.0 + speeds))
    eastward = jnp.broadcast_to(eastward, spectra.shape)
    for _ in range(2):
        ahead = pltpu.roll(spectra, height - 1, 0) - spectra
        behind = pltpu.roll(ahead, 1, 0)
        carried = speeds * (spectra + weight * minmod(ahead, behind))
        flux = jnp.where(eastward, carried, pltpu.roll(carried, height - 1, 0)) * open_faces
        spectra = spectra - (flux - pltpu.roll(flux, 1, 0))
    return spectra


def faces_of(sea):
    return sea * pltpu.roll(sea, sea.shape[0] - 1, 0)


def dot_rows(a, b):
    return lax.dot_general(a, b, (((1,), (1,)), ((), ())), preferred_element_type=jnp.float32)


def kernel(
    n, u_hbm, speed_hbm, sea_hbm, lift_hbm, back_hbm, out_ref,
    u, speed, sea_row, sent, got, cells_u, cells_sea, state, rounded, squared, total, result, lift, back,
    ready, load_sem, own_sem, send_one, recv_one, send_two, recv_two,
):
    me = lax.axis_index("cell")
    depth, cells = u_hbm.shape
    modes, comps = lift.shape
    strips = comps // LANES
    half = n // 2

    barrier = pltpu.get_barrier_semaphore()

    def rank_of(device):
        return device + 1 - 2 * lax.rem(device, 2)

    rank = rank_of(me)

    def greet(k, _):
        pl.semaphore_signal(barrier, inc=1, device_id={"cell": rank_of(k)}, device_id_type=MESH)
        return 0

    lax.fori_loop(rank + 1, n, greet, 0)

    spread = half // GROUP

    def owner_of(tile):
        k = lax.rem(tile, half)
        j, c = lax.rem(k, GROUP), k // GROUP
        return 2 * (j * spread + lax.rem(c + j, spread)) + tile // half

    def tile_of(device):
        chip = device // 2
        j = chip // spread
        c = lax.rem(lax.rem(chip, spread) + GROUP * spread - j, spread)
        return c * GROUP + j + lax.rem(device, 2) * half

    my_tile = tile_of(me)

    head = (GROUP + 1) * LANES
    load_sea = pltpu.make_async_copy(sea_hbm, sea_row, load_sem.at[0])
    load_speed = pltpu.make_async_copy(speed_hbm, speed, load_sem.at[1])
    load_head = pltpu.make_async_copy(u_hbm.at[:, :head], u.at[:, :head], load_sem.at[2])
    load_rest = pltpu.make_async_copy(u_hbm.at[:, head:], u.at[:, head:cells], load_sem.at[3])
    load_lift = pltpu.make_async_copy(lift_hbm, lift, load_sem.at[4])
    load_back = pltpu.make_async_copy(back_hbm, back, load_sem.at[5])
    loads = [load_sea, load_head, load_speed, load_rest, load_lift, load_back]
    for load in loads:
        load.start()

    @pl.when(rank > 0)
    def _():
        pl.semaphore_wait(barrier, rank)

    def answer(k, _):
        pl.semaphore_signal(ready.at[me], inc=1, device_id={"cell": rank_of(k)}, device_id_type=MESH)
        return 0

    lax.fori_loop(0, rank, answer, 0)

    lane = lax.broadcasted_iota(jnp.int32, (EDGE, LANES), 1)
    after = lax.broadcasted_iota(jnp.int32, (EDGE, LANES), 0) < EDGE // 2

    none = jnp.zeros((EDGE, LANES), jnp.float32)
    cells_sea[0:EDGE, :] = none
    cells_sea[cells + EDGE :, :] = none
    cells_u[0:EDGE, :] = none
    u[:, cells:] = jnp.zeros((depth, LANES), jnp.float32)

    load_sea.wait()

    def turn_sea(c, _):
        for j in range(GROUP):
            start = pl.multiple_of((c * GROUP + j) * LANES, LANES)
            row = sea_row[:, pl.ds(start, LANES)].astype(jnp.float32)
            cells_sea[pl.ds(start + EDGE, LANES), :] = jnp.transpose(
                jnp.broadcast_to(row, (LANES, LANES))
            )
        return 0

    lax.fori_loop(0, n // GROUP, turn_sea, 0)
    load_speed.wait()

    place = me * depth
    shift = lax.rem(place, LANES)
    row = place // LANES
    row_after = jnp.minimum(row + 1, strips - 1)
    own_speeds = jnp.where(
        lane < LANES - shift,
        pltpu.roll(jnp.broadcast_to(speed[pl.ds(row, 1), :], (EDGE, LANES)), lax.rem(LANES - shift, LANES), 1),
        pltpu.roll(jnp.broadcast_to(speed[pl.ds(row_after, 1), :], (EDGE, LANES)), lax.rem(LANES - shift, LANES), 1),
    )[0:1, :]

    def turn_tile(tile):
        start = pl.multiple_of(tile * LANES, LANES)
        block = u[:, pl.ds(start, LANES)]
        if depth < LANES:
            block = jnp.concatenate([block, jnp.zeros((LANES - depth, LANES), jnp.float32)], axis=0)
        cells_u[pl.ds(start + EDGE, LANES), :] = jnp.transpose(block)

    def make_group(c):
        for j in range(1, GROUP + 1):
            turn_tile(c * GROUP + j)
        for j in range(GROUP):
            tile = c * GROUP + j
            span = pl.ds(pl.multiple_of(tile * LANES, LANES), LANES + 2 * EDGE)
            block = step_pair(cells_u[span, :], faces_of(cells_sea[span, :]), own_speeds)
            sent[tile, 0:depth, :] = jnp.transpose(block[EDGE : EDGE + LANES, :])[0:depth, :]
            edge = jnp.where(after, block[EDGE + LANES :, :], block[:EDGE, :])
            sent[tile, depth:, :] = pltpu.roll(edge, shift, 1)

    def first(tile, dest, source):
        return pltpu.make_async_remote_copy(
            src_ref=sent.at[tile], dst_ref=got.at[source],
            send_sem=send_one.at[tile], recv_sem=recv_one.at[source],
            device_id={"cell": dest}, device_id_type=MESH,
        )

    def send_group(c):
        for j in range(GROUP):
            tile = c * GROUP + j
            dest = owner_of(tile)

            @pl.when(rank_of(dest) < rank)
            def _():
                first(tile, dest, me).start()

    load_head.wait()
    turn_tile(0)
    make_group(0)
    send_group(0)
    load_rest.wait()

    def next_group(c, _):
        make_group(c)
        send_group(c)
        return 0

    lax.fori_loop(1, n // GROUP, next_group, 0)

    def send_up(k, _):
        spot = lax.rem(k, half)
        tile = k // half * half + lax.rem(spot, spread) * GROUP + spot // spread
        dest = owner_of(tile)

        @pl.when(rank_of(dest) > rank)
        def _():
            pl.semaphore_wait(ready.at[dest], 1)
            first(tile, dest, me).start()

        return 0

    lax.fori_loop(0, n, send_up, 0)

    got[me] = sent[my_tile]
    start = pl.multiple_of(my_tile * LANES, LANES)
    near_sea = [
        cells_sea[pl.ds(start + EDGE, LANES), :],
        jnp.where(after, cells_sea[pl.ds(start + EDGE + LANES, EDGE), :], cells_sea[pl.ds(start, EDGE), :]),
    ]
    near_open = faces_of(jnp.concatenate(near_sea, axis=0))

    def pull(k, _):
        source = lax.rem(me + k, n)
        first(0, source, source).wait_recv()
        return 0

    lax.fori_loop(1, n, pull, 0)

    height = LANES + EDGE
    for q in range(strips):
        low, high = q * LANES, (q + 1) * LANES
        pieces, edge = [], None
        for source in range(low // depth, -(-high // depth)):
            base = source * depth
            pieces.append(got[source, max(low - base, 0) : min(high - base, depth), :])
            mine = got[source, depth:, :]
            edge = mine if edge is None else jnp.where(lane >= base - low, mine, edge)
        block = jnp.concatenate([jnp.transpose(jnp.concatenate(pieces, axis=0)), edge], axis=0)
        state[q] = block
        rounded[:, low:high] = jnp.concatenate([block, none], axis=0).astype(jnp.bfloat16)

    load_lift.wait()
    lifted = dot_rows(rounded[...], lift[...])
    squared[...] = (lifted * lifted).astype(jnp.bfloat16)
    load_back.wait()

    parts = max(k for k in (4, 3, 2, 1) if strips % k == 0)
    wide = strips // parts
    for part in range(parts):
        rows = slice(part * wide * LANES, (part + 1) * wide * LANES)
        source = dot_rows(squared[...], back[rows, :])
        for k in range(wide):
            q = part * wide + k
            block = state[q] + coupling * source[:height, k * LANES : (k + 1) * LANES]
            block = step_pair(block, near_open, speed[q : q + 1, :])[:LANES, :]
            rounded[:LANES, q * LANES : (q + 1) * LANES] = block.astype(jnp.bfloat16)
            total[q * LANES : (q + 1) * LANES, :] = jnp.transpose(block)

    lifted = dot_rows(rounded[:LANES, :], lift[...])
    squared[:LANES, :] = (lifted * lifted).astype(jnp.bfloat16)

    def column(tile):
        return out_ref.at[:, pl.ds(pl.multiple_of(tile * LANES, LANES), LANES)]

    def second(dest, source):
        return pltpu.make_async_remote_copy(
            src_ref=result.at[dest], dst_ref=column(tile_of(source)),
            send_sem=send_two.at[dest], recv_sem=recv_two.at[source],
            device_id={"cell": dest}, device_id_type=MESH,
        )

    own = pltpu.make_async_copy(result.at[me], column(my_tile), own_sem)
    part = n // 4
    comp_part = comps // 4

    def source_two(step, _):
        i = lax.rem(me // part + 1 + step, 4)
        rows = pl.ds(pl.multiple_of(i * comp_part, comp_part), comp_part)
        source = dot_rows(back[rows, :], squared[:LANES, :])
        ended = total[rows, :] + coupling * source
        result[pl.ds(i * part, part)] = ended.reshape(part, depth, LANES)

        def send(j, _):
            dest = i * part + j

            @pl.when(dest != me)
            def _():
                second(dest, me).start()

            return 0

        lax.fori_loop(0, part, send, 0)
        return 0

    lax.fori_loop(0, 4, source_two, 0)
    own.start()

    def finish(k, _):
        dest = lax.rem(me + k, n)
        source = lax.rem(me + n - k, n)
        first(tile_of(dest), dest, me).wait_send()
        second(dest, me).wait_send()
        second(source, source).wait_recv()
        return 0

    lax.fori_loop(1, n, finish, 0)
    own.wait()


def shards(wave_energy, courant, sea_mask, lift_weight, back_weight):
    n = lax.axis_size("cell")
    groups, cells = wave_energy.shape
    modes = lift_weight.shape[0]
    depth = -(-groups // 8) * 8
    extra = depth - groups
    if extra:
        wave_energy = jnp.pad(wave_energy, ((0, extra), (0, 0)))
        courant = jnp.pad(courant.reshape(n, groups), ((0, 0), (0, extra))).reshape(-1)
        lift_weight = jnp.pad(
            lift_weight.reshape(modes, n, groups), ((0, 0), (0, 0), (0, extra))
        ).reshape(modes, n * depth)
        back_weight = jnp.pad(
            back_weight.reshape(n, groups, modes), ((0, 0), (0, extra), (0, 0))
        ).reshape(n * depth, modes)
    comps = n * depth
    strips = comps // LANES
    tall = LANES + 2 * EDGE
    buffers = [
        pltpu.VMEM((depth, cells + LANES), jnp.float32),
        pltpu.VMEM((strips, LANES), jnp.float32),
        pltpu.VMEM((1, cells), jnp.int32),
        pltpu.VMEM((n, depth + EDGE, LANES), jnp.float32),
        pltpu.VMEM((n, depth + EDGE, LANES), jnp.float32),
        pltpu.VMEM((cells + LANES + EDGE, LANES), jnp.float32),
        pltpu.VMEM((cells + 2 * EDGE, LANES), jnp.float32),
        pltpu.VMEM((strips, LANES + EDGE, LANES), jnp.float32),
        pltpu.VMEM((tall, comps), jnp.bfloat16),
        pltpu.VMEM((tall, modes), jnp.bfloat16),
        pltpu.VMEM((comps, LANES), jnp.float32),
        pltpu.VMEM((n, depth, LANES), jnp.float32),
        pltpu.VMEM((modes, comps), jnp.bfloat16),
        pltpu.VMEM((comps, modes), jnp.bfloat16),
    ]
    held = sum(math.prod(b.shape) * jnp.dtype(b.dtype).itemsize for b in buffers)
    operands = [
        pltpu.with_memory_space_constraint(x, pltpu.HBM)
        for x in (wave_energy, courant.reshape(strips, LANES), sea_mask[None, :], lift_weight, back_weight)
    ]
    out = pl.pallas_call(
        functools.partial(kernel, n),
        out_shape=jax.ShapeDtypeStruct((depth, cells), jnp.float32),
        in_specs=[pl.BlockSpec(memory_space=pltpu.HBM)] * 5,
        out_specs=pl.BlockSpec(memory_space=pl.ANY),
        scratch_shapes=buffers
        + [
            pltpu.SemaphoreType.REGULAR((n,)),
            pltpu.SemaphoreType.DMA((6,)),
            pltpu.SemaphoreType.DMA,
            pltpu.SemaphoreType.DMA((n,)),
            pltpu.SemaphoreType.DMA((n,)),
            pltpu.SemaphoreType.DMA((n,)),
            pltpu.SemaphoreType.DMA((n,)),
        ],
        compiler_params=pltpu.CompilerParams(
            collective_id=0, has_side_effects=True, vmem_limit_bytes=held + 4 * 1024 * 1024
        ),
    )(*operands)
    return out[:groups]


def solution(mesh):
    placed = (P(("member", "cell"), None), P(), P(), P(), P())
    return jax.shard_map(
        shards, mesh=mesh, in_specs=placed, out_specs=P(("member", "cell"), None), check_vma=False
    )
```

```python
import functools
import math

import jax
import jax.numpy as jnp
from jax import lax
from jax.experimental import pallas as pl
from jax.experimental.pallas import tpu as pltpu
from jax.sharding import PartitionSpec as P

LANES = 128
EDGE = 8
GROUP = 4
MESH = pl.DeviceIdType.MESH

coupling = 0.25


def minmod(first_term, second_term):
    low = jnp.minimum(first_term, second_term)
    high = jnp.maximum(first_term, second_term)
    return jnp.maximum(low, 0.0) + jnp.minimum(high, 0.0)


def step_pair(spectra, open_faces, speeds):
    height = spectra.shape[0]
    eastward = speeds >= 0.0
    weight = jnp.where(eastward, 0.5 * (1.0 - speeds), -0.5 * (1.0 + speeds))
    eastward = jnp.broadcast_to(eastward, spectra.shape)
    for _ in range(2):
        ahead = pltpu.roll(spectra, height - 1, 0) - spectra
        behind = pltpu.roll(ahead, 1, 0)
        carried = speeds * (spectra + weight * minmod(ahead, behind))
        flux = jnp.where(eastward, carried, pltpu.roll(carried, height - 1, 0)) * open_faces
        spectra = spectra - (flux - pltpu.roll(flux, 1, 0))
    return spectra


def faces_of(sea):
    return sea * pltpu.roll(sea, sea.shape[0] - 1, 0)


def dot_rows(a, b):
    return lax.dot_general(a, b, (((1,), (1,)), ((), ())), preferred_element_type=jnp.float32)


def kernel(
    n, u_hbm, speed_hbm, sea_hbm, lift_hbm, back_hbm, out_ref,
    u, speed, sea_row, sent, got, cells_u, cells_sea, state, rounded, squared, total, result, lift, back,
    ready, load_sem, own_sem, send_one, recv_one, send_two, recv_two,
):
    me = lax.axis_index("cell")
    depth, cells = u_hbm.shape
    modes, comps = lift.shape
    strips = comps // LANES
    half = n // 2

    barrier = pltpu.get_barrier_semaphore()

    def rank_of(device):
        return device + 1 - 2 * lax.rem(device, 2)

    rank = rank_of(me)

    def greet(k, _):
        pl.semaphore_signal(barrier, inc=1, device_id={"cell": rank_of(k)}, device_id_type=MESH)
        return 0

    lax.fori_loop(rank + 1, n, greet, 0)

    spread = half // GROUP

    def owner_of(tile):
        k = lax.rem(tile, half)
        j, c = lax.rem(k, GROUP), k // GROUP
        return 2 * (j * spread + lax.rem(c + j, spread)) + tile // half

    def tile_of(device):
        chip = device // 2
        j = chip // spread
        c = lax.rem(lax.rem(chip, spread) + GROUP * spread - j, spread)
        return c * GROUP + j + lax.rem(device, 2) * half

    my_tile = tile_of(me)

    head = (GROUP + 1) * LANES
    load_sea = pltpu.make_async_copy(sea_hbm, sea_row, load_sem.at[0])
    load_speed = pltpu.make_async_copy(speed_hbm, speed, load_sem.at[1])
    load_head = pltpu.make_async_copy(u_hbm.at[:, :head], u.at[:, :head], load_sem.at[2])
    load_rest = pltpu.make_async_copy(u_hbm.at[:, head:], u.at[:, head:cells], load_sem.at[3])
    load_lift = pltpu.make_async_copy(lift_hbm, lift, load_sem.at[4])
    load_back = pltpu.make_async_copy(back_hbm, back, load_sem.at[5])
    loads = [load_sea, load_head, load_speed, load_rest, load_lift, load_back]
    for load in loads:
        load.start()

    @pl.when(rank > 0)
    def _():
        pl.semaphore_wait(barrier, rank)

    def answer(k, _):
        pl.semaphore_signal(ready.at[me], inc=1, device_id={"cell": rank_of(k)}, device_id_type=MESH)
        return 0

    lax.fori_loop(0, rank, answer, 0)

    lane = lax.broadcasted_iota(jnp.int32, (EDGE, LANES), 1)
    after = lax.broadcasted_iota(jnp.int32, (EDGE, LANES), 0) < EDGE // 2

    none = jnp.zeros((EDGE, LANES), jnp.float32)
    cells_sea[0:EDGE, :] = none
    cells_sea[cells + EDGE :, :] = none
    cells_u[0:EDGE, :] = none
    u[:, cells:] = jnp.zeros((depth, LANES), jnp.float32)

    load_sea.wait()

    def turn_sea(c, _):
        for j in range(GROUP):
            start = pl.multiple_of((c * GROUP + j) * LANES, LANES)
            row = sea_row[:, pl.ds(start, LANES)].astype(jnp.float32)
            cells_sea[pl.ds(start + EDGE, LANES), :] = jnp.transpose(
                jnp.broadcast_to(row, (LANES, LANES))
            )
        return 0

    lax.fori_loop(0, n // GROUP, turn_sea, 0)
    load_speed.wait()

    place = me * depth
    shift = lax.rem(place, LANES)
    row = place // LANES
    row_after = jnp.minimum(row + 1, strips - 1)
    own_speeds = jnp.where(
        lane < LANES - shift,
        pltpu.roll(jnp.broadcast_to(speed[pl.ds(row, 1), :], (EDGE, LANES)), lax.rem(LANES - shift, LANES), 1),
        pltpu.roll(jnp.broadcast_to(speed[pl.ds(row_after, 1), :], (EDGE, LANES)), lax.rem(LANES - shift, LANES), 1),
    )[0:1, :]

    def turn_tile(tile):
        start = pl.multiple_of(tile * LANES, LANES)
        block = u[:, pl.ds(start, LANES)]
        if depth < LANES:
            block = jnp.concatenate([block, jnp.zeros((LANES - depth, LANES), jnp.float32)], axis=0)
        cells_u[pl.ds(start + EDGE, LANES), :] = jnp.transpose(block)

    def make_group(c):
        for j in range(1, GROUP + 1):
            turn_tile(c * GROUP + j)
        for j in range(GROUP):
            tile = c * GROUP + j
            span = pl.ds(pl.multiple_of(tile * LANES, LANES), LANES + 2 * EDGE)
            block = step_pair(cells_u[span, :], faces_of(cells_sea[span, :]), own_speeds)
            sent[tile, 0:depth, :] = jnp.transpose(block[EDGE : EDGE + LANES, :])[0:depth, :]
            edge = jnp.where(after, block[EDGE + LANES :, :], block[:EDGE, :])
            sent[tile, depth:, :] = pltpu.roll(edge, shift, 1)

    def first(tile, dest, source):
        return pltpu.make_async_remote_copy(
            src_ref=sent.at[tile], dst_ref=got.at[source],
            send_sem=send_one.at[tile], recv_sem=recv_one.at[source],
            device_id={"cell": dest}, device_id_type=MESH,
        )

    def send_group(c):
        for j in range(GROUP):
            tile = c * GROUP + j
            dest = owner_of(tile)

            @pl.when(rank_of(dest) < rank)
            def _():
                first(tile, dest, me).start()

    def next_group(c, _):
        make_group(c)
        send_group(c)
        return 0

    def send_up(k, _):
        spot = lax.rem(k, half)
        tile = k // half * half + lax.rem(spot, spread) * GROUP + spot // spread
        dest = owner_of(tile)

        @pl.when(rank_of(dest) > rank)
        def _():
            pl.semaphore_wait(ready.at[dest], 1)
            first(tile, dest, me).start()

        return 0

    load_head.wait()
    turn_tile(0)
    next_group(0, 0)
    load_rest.wait()
    lax.fori_loop(1, spread, next_group, 0)
    lax.fori_loop(0, half, send_up, 0)
    lax.fori_loop(spread, 2 * spread, next_group, 0)
    lax.fori_loop(half, n, send_up, 0)

    got[me] = sent[my_tile]
    start = pl.multiple_of(my_tile * LANES, LANES)
    near_sea = [
        cells_sea[pl.ds(start + EDGE, LANES), :],
        jnp.where(after, cells_sea[pl.ds(start + EDGE + LANES, EDGE), :], cells_sea[pl.ds(start, EDGE), :]),
    ]
    near_open = faces_of(jnp.concatenate(near_sea, axis=0))

    def pull(k, _):
        source = lax.rem(me + k, n)
        first(0, source, source).wait_recv()
        return 0

    lax.fori_loop(1, n, pull, 0)

    height = LANES + EDGE
    for q in range(strips):
        low, high = q * LANES, (q + 1) * LANES
        pieces, edge = [], None
        for source in range(low // depth, -(-high // depth)):
            base = source * depth
            pieces.append(got[source, max(low - base, 0) : min(high - base, depth), :])
            mine = got[source, depth:, :]
            edge = mine if edge is None else jnp.where(lane >= base - low, mine, edge)
        block = jnp.concatenate([jnp.transpose(jnp.concatenate(pieces, axis=0)), edge], axis=0)
        state[q] = block
        rounded[:, low:high] = jnp.concatenate([block, none], axis=0).astype(jnp.bfloat16)

    load_lift.wait()
    lifted = dot_rows(rounded[...], lift[...])
    squared[...] = (lifted * lifted).astype(jnp.bfloat16)
    load_back.wait()

    parts = max(k for k in (4, 3, 2, 1) if strips % k == 0)
    wide = strips // parts
    for part in range(parts):
        rows = slice(part * wide * LANES, (part + 1) * wide * LANES)
        source = dot_rows(squared[...], back[rows, :])
        for k in range(wide):
            q = part * wide + k
            block = state[q] + coupling * source[:height, k * LANES : (k + 1) * LANES]
            block = step_pair(block, near_open, speed[q : q + 1, :])[:LANES, :]
            rounded[:LANES, q * LANES : (q + 1) * LANES] = block.astype(jnp.bfloat16)
            total[q * LANES : (q + 1) * LANES, :] = jnp.transpose(block)

    lifted = dot_rows(rounded[:LANES, :], lift[...])
    squared[:LANES, :] = (lifted * lifted).astype(jnp.bfloat16)

    def column(tile):
        return out_ref.at[:, pl.ds(pl.multiple_of(tile * LANES, LANES), LANES)]

    def second(dest, source):
        return pltpu.make_async_remote_copy(
            src_ref=result.at[dest], dst_ref=column(tile_of(source)),
            send_sem=send_two.at[dest], recv_sem=recv_two.at[source],
            device_id={"cell": dest}, device_id_type=MESH,
        )

    own = pltpu.make_async_copy(result.at[me], column(my_tile), own_sem)
    part = n // 4
    comp_part = comps // 4

    def source_two(step, _):
        i = lax.rem(me // part + 1 + step, 4)
        rows = pl.ds(pl.multiple_of(i * comp_part, comp_part), comp_part)
        source = dot_rows(back[rows, :], squared[:LANES, :])
        ended = total[rows, :] + coupling * source
        result[pl.ds(i * part, part)] = ended.reshape(part, depth, LANES)

        def send(j, _):
            dest = i * part + j

            @pl.when(dest != me)
            def _():
                second(dest, me).start()

            return 0

        lax.fori_loop(0, part, send, 0)
        return 0

    lax.fori_loop(0, 4, source_two, 0)
    own.start()

    def finish(k, _):
        dest = lax.rem(me + k, n)
        source = lax.rem(me + n - k, n)
        first(tile_of(dest), dest, me).wait_send()
        second(dest, me).wait_send()
        second(source, source).wait_recv()
        return 0

    lax.fori_loop(1, n, finish, 0)
    own.wait()


def shards(wave_energy, courant, sea_mask, lift_weight, back_weight):
    n = lax.axis_size("cell")
    groups, cells = wave_energy.shape
    modes = lift_weight.shape[0]
    depth = -(-groups // 8) * 8
    extra = depth - groups
    if extra:
        wave_energy = jnp.pad(wave_energy, ((0, extra), (0, 0)))
        courant = jnp.pad(courant.reshape(n, groups), ((0, 0), (0, extra))).reshape(-1)
        lift_weight = jnp.pad(
            lift_weight.reshape(modes, n, groups), ((0, 0), (0, 0), (0, extra))
        ).reshape(modes, n * depth)
        back_weight = jnp.pad(
            back_weight.reshape(n, groups, modes), ((0, 0), (0, extra), (0, 0))
        ).reshape(n * depth, modes)
    comps = n * depth
    strips = comps // LANES
    tall = LANES + 2 * EDGE
    buffers = [
        pltpu.VMEM((depth, cells + LANES), jnp.float32),
        pltpu.VMEM((strips, LANES), jnp.float32),
        pltpu.VMEM((1, cells), jnp.int32),
        pltpu.VMEM((n, depth + EDGE, LANES), jnp.float32),
        pltpu.VMEM((n, depth + EDGE, LANES), jnp.float32),
        pltpu.VMEM((cells + LANES + EDGE, LANES), jnp.float32),
        pltpu.VMEM((cells + 2 * EDGE, LANES), jnp.float32),
        pltpu.VMEM((strips, LANES + EDGE, LANES), jnp.float32),
        pltpu.VMEM((tall, comps), jnp.bfloat16),
        pltpu.VMEM((tall, modes), jnp.bfloat16),
        pltpu.VMEM((comps, LANES), jnp.float32),
        pltpu.VMEM((n, depth, LANES), jnp.float32),
        pltpu.VMEM((modes, comps), jnp.bfloat16),
        pltpu.VMEM((comps, modes), jnp.bfloat16),
    ]
    held = sum(math.prod(b.shape) * jnp.dtype(b.dtype).itemsize for b in buffers)
    operands = [
        pltpu.with_memory_space_constraint(x, pltpu.HBM)
        for x in (wave_energy, courant.reshape(strips, LANES), sea_mask[None, :], lift_weight, back_weight)
    ]
    out = pl.pallas_call(
        functools.partial(kernel, n),
        out_shape=jax.ShapeDtypeStruct((depth, cells), jnp.float32),
        in_specs=[pl.BlockSpec(memory_space=pltpu.HBM)] * 5,
        out_specs=pl.BlockSpec(memory_space=pl.ANY),
        scratch_shapes=buffers
        + [
            pltpu.SemaphoreType.REGULAR((n,)),
            pltpu.SemaphoreType.DMA((6,)),
            pltpu.SemaphoreType.DMA,
            pltpu.SemaphoreType.DMA((n,)),
            pltpu.SemaphoreType.DMA((n,)),
            pltpu.SemaphoreType.DMA((n,)),
            pltpu.SemaphoreType.DMA((n,)),
        ],
        compiler_params=pltpu.CompilerParams(
            collective_id=0, has_side_effects=True, vmem_limit_bytes=held + 4 * 1024 * 1024
        ),
    )(*operands)
    return out[:groups]


def solution(mesh):
    placed = (P(("member", "cell"), None), P(), P(), P(), P())
    return jax.shard_map(
        shards, mesh=mesh, in_specs=placed, out_specs=P(("member", "cell"), None), check_vma=False
    )
```

```python
import functools
import math

import jax
import jax.numpy as jnp
from jax import lax
from jax.experimental import pallas as pl
from jax.experimental.pallas import tpu as pltpu
from jax.sharding import PartitionSpec as P

LANES = 128
EDGE = 8
GROUP = 4
MESH = pl.DeviceIdType.MESH

coupling = 0.25


def minmod(first_term, second_term):
    low = jnp.minimum(first_term, second_term)
    high = jnp.maximum(first_term, second_term)
    return jnp.maximum(low, 0.0) + jnp.minimum(high, 0.0)


def step_pair(spectra, open_faces, speeds):
    height = spectra.shape[0]
    eastward = speeds >= 0.0
    weight = jnp.where(eastward, 0.5 * (1.0 - speeds), -0.5 * (1.0 + speeds))
    eastward = jnp.broadcast_to(eastward, spectra.shape)
    for _ in range(2):
        ahead = pltpu.roll(spectra, height - 1, 0) - spectra
        behind = pltpu.roll(ahead, 1, 0)
        carried = speeds * (spectra + weight * minmod(ahead, behind))
        flux = jnp.where(eastward, carried, pltpu.roll(carried, height - 1, 0)) * open_faces
        spectra = spectra - (flux - pltpu.roll(flux, 1, 0))
    return spectra


def faces_of(sea):
    return sea * pltpu.roll(sea, sea.shape[0] - 1, 0)


def dot_rows(a, b):
    return lax.dot_general(a, b, (((1,), (1,)), ((), ())), preferred_element_type=jnp.float32)


def kernel(
    n, u_hbm, speed_hbm, sea_hbm, lift_hbm, back_hbm, out_ref,
    u, speed, sea_row, sent, got, cells_u, cells_sea, state, rounded, squared, total, result, beside, lift, back,
    load_sem, own_sem, send_one, recv_one, send_two, recv_two, send_border, recv_border,
):
    me = lax.axis_index("cell")
    depth, cells = u_hbm.shape
    modes, comps = lift.shape
    strips = comps // LANES
    half = n // 2

    barrier = pltpu.get_barrier_semaphore()

    def greet(k, _):
        other = lax.rem(me + k + half, n)

        @pl.when(other != me)
        def _():
            pl.semaphore_signal(barrier, inc=1, device_id={"cell": other}, device_id_type=MESH)

        return 0

    lax.fori_loop(0, n, greet, 0)

    spread = half // GROUP
    leading = lax.rem(me, 2) == 0

    def tile_in(group, j):
        return 2 * (j * spread + lax.rem(lax.rem(group, spread) + j, spread)) + group // spread

    load_sea = pltpu.make_async_copy(sea_hbm, sea_row, load_sem.at[0])
    load_speed = pltpu.make_async_copy(speed_hbm, speed, load_sem.at[1])
    load_u = pltpu.make_async_copy(u_hbm, u, load_sem.at[2])
    load_lift = pltpu.make_async_copy(lift_hbm, lift, load_sem.at[3])
    load_back = pltpu.make_async_copy(back_hbm, back, load_sem.at[4])
    loads = [load_sea, load_u, load_speed, load_lift, load_back]
    for load in loads:
        load.start()

    lane = lax.broadcasted_iota(jnp.int32, (EDGE, LANES), 1)
    after = lax.broadcasted_iota(jnp.int32, (EDGE, LANES), 0) < EDGE // 2

    none = jnp.zeros((EDGE, LANES), jnp.float32)
    cells_sea[0:EDGE, :] = none
    cells_sea[cells + EDGE :, :] = none
    cells_u[0:EDGE, :] = none
    cells_u[cells + EDGE :, :] = none

    load_sea.wait()

    def turn_sea(c, _):
        for j in range(GROUP):
            start = pl.multiple_of((c * GROUP + j) * LANES, LANES)
            row = sea_row[:, pl.ds(start, LANES)].astype(jnp.float32)
            cells_sea[pl.ds(start + EDGE, LANES), :] = jnp.transpose(
                jnp.broadcast_to(row, (LANES, LANES))
            )
        return 0

    lax.fori_loop(0, n // GROUP, turn_sea, 0)
    load_speed.wait()

    place = me * depth
    shift = lax.rem(place, LANES)
    row = place // LANES
    row_after = jnp.minimum(row + 1, strips - 1)
    own_speeds = jnp.where(
        lane < LANES - shift,
        pltpu.roll(jnp.broadcast_to(speed[pl.ds(row, 1), :], (EDGE, LANES)), lax.rem(LANES - shift, LANES), 1),
        pltpu.roll(jnp.broadcast_to(speed[pl.ds(row_after, 1), :], (EDGE, LANES)), lax.rem(LANES - shift, LANES), 1),
    )[0:1, :]

    load_u.wait()

    def turn_tiles(c, _):
        for j in range(GROUP):
            start = pl.multiple_of((c * GROUP + j) * LANES, LANES)
            block = u[:, pl.ds(start, LANES)]
            if depth < LANES:
                rest = jnp.zeros((LANES - depth, LANES), jnp.float32)
                block = jnp.concatenate([block, rest], axis=0)
            cells_u[pl.ds(start + EDGE, LANES), :] = jnp.transpose(block)
        return 0

    lax.fori_loop(0, n // GROUP, turn_tiles, 0)

    def make_group(group):
        for j in range(GROUP):
            tile = tile_in(group, j)
            span = pl.ds(pl.multiple_of(tile * LANES, LANES), LANES + 2 * EDGE)
            block = step_pair(cells_u[span, :], faces_of(cells_sea[span, :]), own_speeds)
            sent[tile, 0:depth, :] = jnp.transpose(block[EDGE : EDGE + LANES, :])[0:depth, :]
            edge = jnp.where(after, block[EDGE + LANES :, :], block[:EDGE, :])
            sent[tile, depth:, :] = pltpu.roll(edge, shift, 1)

    def first(dest, source, rows):
        return pltpu.make_async_remote_copy(
            src_ref=sent.at[dest, 0:rows], dst_ref=got.at[source, 0:rows],
            send_sem=send_one.at[dest], recv_sem=recv_one.at[source],
            device_id={"cell": dest}, device_id_type=MESH,
        )

    def send_groups(groups, rows):
        def body(group, _):
            make_group(group)
            for j in range(GROUP):
                dest = tile_in(group, j)

                @pl.when(dest != me)
                def _():
                    first(dest, me, rows).start()

            return 0

        lax.fori_loop(*groups, body, 0)

    pl.semaphore_wait(barrier, n - 1)
    send_groups((0, spread), depth + EDGE)
    send_groups((spread, 2 * spread), depth)

    got[me] = sent[me]
    start = pl.multiple_of(me * LANES, LANES)
    near_sea = [
        cells_sea[pl.ds(start + EDGE, LANES), :],
        jnp.where(after, cells_sea[pl.ds(start + EDGE + LANES, EDGE), :], cells_sea[pl.ds(start, EDGE), :]),
    ]
    near_open = faces_of(jnp.concatenate(near_sea, axis=0))

    def pull(rows):
        def body(k, _):
            source = lax.rem(me + k, n)
            first(source, source, rows).wait_recv()
            return 0

        lax.fori_loop(1, n, body, 0)

    @pl.when(leading)
    def _():
        pull(depth + EDGE)

    @pl.when(jnp.logical_not(leading))
    def _():
        pull(depth)

    for q in range(strips):
        low, high = q * LANES, (q + 1) * LANES
        pieces = []
        for source in range(low // depth, -(-high // depth)):
            base = source * depth
            pieces.append(got[source, max(low - base, 0) : min(high - base, depth), :])
        block = jnp.transpose(jnp.concatenate(pieces, axis=0))
        state[q, :LANES, :] = block
        rounded[:LANES, low:high] = block.astype(jnp.bfloat16)

    def border(side):
        return pltpu.make_async_remote_copy(
            src_ref=state.at[:, 0:EDGE] if side else state.at[:, LANES - EDGE : LANES],
            dst_ref=beside.at[side], send_sem=send_border.at[side], recv_sem=recv_border.at[side],
            device_id={"cell": me - 1 if side else me + 1}, device_id_type=MESH,
        )

    @pl.when(leading)
    def _():
        border(0).start()

        @pl.when(me > 0)
        def _():
            border(1).start()

    @pl.when(jnp.logical_not(leading))
    def _():
        border(0).wait_recv()

        @pl.when(me < n - 1)
        def _():
            border(1).wait_recv()

        @pl.when(me == n - 1)
        def _():
            beside[1] = jnp.zeros((strips, EDGE, LANES), jnp.float32)

    height = LANES + EDGE
    for q in range(strips):
        low, high = q * LANES, (q + 1) * LANES
        edge = None
        for source in range(low // depth, -(-high // depth)):
            mine = got[source, depth:, :]
            edge = mine if edge is None else jnp.where(lane >= source * depth - low, mine, edge)
        edge = jnp.where(leading, edge, jnp.where(after, beside[1, q], beside[0, q]))
        state[q, LANES:, :] = edge
        rounded[LANES:, low:high] = jnp.concatenate([edge, none], axis=0).astype(jnp.bfloat16)

    load_lift.wait()
    lifted = dot_rows(rounded[...], lift[...])
    squared[...] = (lifted * lifted).astype(jnp.bfloat16)
    load_back.wait()

    parts = max(k for k in (4, 3, 2, 1) if strips % k == 0)
    wide = strips // parts
    for part in range(parts):
        rows = slice(part * wide * LANES, (part + 1) * wide * LANES)
        source = dot_rows(squared[...], back[rows, :])
        for k in range(wide):
            q = part * wide + k
            block = state[q] + coupling * source[:height, k * LANES : (k + 1) * LANES]
            block = step_pair(block, near_open, speed[q : q + 1, :])[:LANES, :]
            rounded[:LANES, q * LANES : (q + 1) * LANES] = block.astype(jnp.bfloat16)
            total[q * LANES : (q + 1) * LANES, :] = jnp.transpose(block)

    lifted = dot_rows(rounded[:LANES, :], lift[...])
    squared[:LANES, :] = (lifted * lifted).astype(jnp.bfloat16)

    def column(tile):
        return out_ref.at[:, pl.ds(pl.multiple_of(tile * LANES, LANES), LANES)]

    def second(dest, source):
        return pltpu.make_async_remote_copy(
            src_ref=result.at[dest], dst_ref=column(source),
            send_sem=send_two.at[dest], recv_sem=recv_two.at[source],
            device_id={"cell": dest}, device_id_type=MESH,
        )

    own = pltpu.make_async_copy(result.at[me], column(me), own_sem)
    part = n // 4
    comp_part = comps // 4

    def source_two(step, _):
        i = lax.rem(me // part + 1 + step, 4)
        rows = pl.ds(pl.multiple_of(i * comp_part, comp_part), comp_part)
        source = dot_rows(back[rows, :], squared[:LANES, :])
        ended = total[rows, :] + coupling * source
        result[pl.ds(i * part, part)] = ended.reshape(part, depth, LANES)

        def send(j, _):
            dest = i * part + j

            @pl.when(dest != me)
            def _():
                second(dest, me).start()

            return 0

        lax.fori_loop(0, part, send, 0)
        return 0

    lax.fori_loop(0, 4, source_two, 0)
    own.start()

    def finish(k, _):
        dest = lax.rem(me + k, n)
        source = lax.rem(me + n - k, n)

        @pl.when(lax.rem(dest, 2) == 0)
        def _():
            first(dest, me, depth + EDGE).wait_send()

        @pl.when(lax.rem(dest, 2) == 1)
        def _():
            first(dest, me, depth).wait_send()

        second(dest, me).wait_send()
        second(source, source).wait_recv()
        return 0

    lax.fori_loop(1, n, finish, 0)

    @pl.when(leading)
    def _():
        border(0).wait_send()

        @pl.when(me > 0)
        def _():
            border(1).wait_send()

    own.wait()


def shards(wave_energy, courant, sea_mask, lift_weight, back_weight):
    n = lax.axis_size("cell")
    groups, cells = wave_energy.shape
    modes = lift_weight.shape[0]
    depth = -(-groups // 8) * 8
    extra = depth - groups
    if extra:
        wave_energy = jnp.pad(wave_energy, ((0, extra), (0, 0)))
        courant = jnp.pad(courant.reshape(n, groups), ((0, 0), (0, extra))).reshape(-1)
        lift_weight = jnp.pad(
            lift_weight.reshape(modes, n, groups), ((0, 0), (0, 0), (0, extra))
        ).reshape(modes, n * depth)
        back_weight = jnp.pad(
            back_weight.reshape(n, groups, modes), ((0, 0), (0, extra), (0, 0))
        ).reshape(n * depth, modes)
    comps = n * depth
    strips = comps // LANES
    tall = LANES + 2 * EDGE
    buffers = [
        pltpu.VMEM((depth, cells), jnp.float32),
        pltpu.VMEM((strips, LANES), jnp.float32),
        pltpu.VMEM((1, cells), jnp.int32),
        pltpu.VMEM((n, depth + EDGE, LANES), jnp.float32),
        pltpu.VMEM((n, depth + EDGE, LANES), jnp.float32),
        pltpu.VMEM((cells + 2 * EDGE, LANES), jnp.float32),
        pltpu.VMEM((cells + 2 * EDGE, LANES), jnp.float32),
        pltpu.VMEM((strips, LANES + EDGE, LANES), jnp.float32),
        pltpu.VMEM((tall, comps), jnp.bfloat16),
        pltpu.VMEM((tall, modes), jnp.bfloat16),
        pltpu.VMEM((comps, LANES), jnp.float32),
        pltpu.VMEM((n, depth, LANES), jnp.float32),
        pltpu.VMEM((2, strips, EDGE, LANES), jnp.float32),
        pltpu.VMEM((modes, comps), jnp.bfloat16),
        pltpu.VMEM((comps, modes), jnp.bfloat16),
    ]
    held = sum(math.prod(b.shape) * jnp.dtype(b.dtype).itemsize for b in buffers)
    operands = [
        pltpu.with_memory_space_constraint(x, pltpu.HBM)
        for x in (wave_energy, courant.reshape(strips, LANES), sea_mask[None, :], lift_weight, back_weight)
    ]
    out = pl.pallas_call(
        functools.partial(kernel, n),
        out_shape=jax.ShapeDtypeStruct((depth, cells), jnp.float32),
        in_specs=[pl.BlockSpec(memory_space=pltpu.HBM)] * 5,
        out_specs=pl.BlockSpec(memory_space=pl.ANY),
        scratch_shapes=buffers
        + [
            pltpu.SemaphoreType.DMA((5,)),
            pltpu.SemaphoreType.DMA,
            pltpu.SemaphoreType.DMA((n,)),
            pltpu.SemaphoreType.DMA((n,)),
            pltpu.SemaphoreType.DMA((n,)),
            pltpu.SemaphoreType.DMA((n,)),
            pltpu.SemaphoreType.DMA((2,)),
            pltpu.SemaphoreType.DMA((2,)),
        ],
        compiler_params=pltpu.CompilerParams(
            collective_id=0, has_side_effects=True, vmem_limit_bytes=held + 4 * 1024 * 1024
        ),
    )(*operands)
    return out[:groups]


def solution(mesh):
    placed = (P(("member", "cell"), None), P(), P(), P(), P())
    return jax.shard_map(
        shards, mesh=mesh, in_specs=placed, out_specs=P(("member", "cell"), None), check_vma=False
    )
```

```python
import functools
import math

import jax
import jax.numpy as jnp
from jax import lax
from jax.experimental import pallas as pl
from jax.experimental.pallas import tpu as pltpu
from jax.sharding import PartitionSpec as P

LANES = 128
EDGE = 8
GROUP = 4
MESH = pl.DeviceIdType.MESH

SERVED = ((1, 0, 2, 3), (2, 3, 0, 1), (3, 0, 1, 2), (0, 1, 2, 3))


def pack(digits):
    return sum(digit << (2 * k) for k, digit in enumerate(digits))


coupling = 0.25


def minmod(first_term, second_term):
    low = jnp.minimum(first_term, second_term)
    high = jnp.maximum(first_term, second_term)
    return jnp.maximum(low, 0.0) + jnp.minimum(high, 0.0)


def step_pair(spectra, open_faces, speeds):
    height = spectra.shape[0]
    eastward = speeds >= 0.0
    weight = jnp.where(eastward, 0.5 * (1.0 - speeds), -0.5 * (1.0 + speeds))
    eastward = jnp.broadcast_to(eastward, spectra.shape)
    for _ in range(2):
        ahead = pltpu.roll(spectra, height - 1, 0) - spectra
        behind = pltpu.roll(ahead, 1, 0)
        carried = speeds * (spectra + weight * minmod(ahead, behind))
        flux = jnp.where(eastward, carried, pltpu.roll(carried, height - 1, 0)) * open_faces
        spectra = spectra - (flux - pltpu.roll(flux, 1, 0))
    return spectra


def faces_of(sea):
    return sea * pltpu.roll(sea, sea.shape[0] - 1, 0)


def dot_rows(a, b):
    return lax.dot_general(a, b, (((1,), (1,)), ((), ())), preferred_element_type=jnp.float32)


def kernel(
    n, u_hbm, speed_hbm, sea_hbm, lift_hbm, back_hbm, out_ref,
    u, speed, sea_row, sent, got, cells_u, cells_sea, state, rounded, squared, total, result, beside, lift, back,
    load_sem, own_sem, send_one, recv_one, send_two, recv_two, send_border, recv_border,
):
    me = lax.axis_index("cell")
    depth, cells = u_hbm.shape
    modes, comps = lift.shape
    strips = comps // LANES
    half = n // 2

    barrier = pltpu.get_barrier_semaphore()

    def greet(k, _):
        @pl.when(k != me)
        def _():
            pl.semaphore_signal(barrier, inc=1, device_id={"cell": k}, device_id_type=MESH)

        return 0

    lax.fori_loop(0, n, greet, 0)

    spread = half // GROUP
    leading = lax.rem(me, 2) == 0

    quarter = n // 4
    mine = me // quarter
    order = jnp.int32(pack(SERVED[3]))
    for k in range(3):
        order = jnp.where(mine == k, pack(SERVED[k]), order)

    def served(step):
        return jnp.right_shift(order, 2 * step) & 3

    def tile_in(group, j):
        return 2 * (j * spread + lax.rem(lax.rem(group, spread) + j, spread)) + group // spread

    load_sea = pltpu.make_async_copy(sea_hbm, sea_row, load_sem.at[0])
    load_speed = pltpu.make_async_copy(speed_hbm, speed, load_sem.at[1])
    load_u = pltpu.make_async_copy(u_hbm, u, load_sem.at[2])
    load_lift = pltpu.make_async_copy(lift_hbm, lift, load_sem.at[3])
    load_back = pltpu.make_async_copy(back_hbm, back, load_sem.at[4])
    loads = [load_sea, load_u, load_speed, load_lift, load_back]
    for load in loads:
        load.start()

    lane = lax.broadcasted_iota(jnp.int32, (EDGE, LANES), 1)
    after = lax.broadcasted_iota(jnp.int32, (EDGE, LANES), 0) < EDGE // 2

    none = jnp.zeros((EDGE, LANES), jnp.float32)
    cells_sea[0:EDGE, :] = none
    cells_sea[cells + EDGE :, :] = none
    cells_u[0:EDGE, :] = none
    cells_u[cells + EDGE :, :] = none

    load_sea.wait()

    def turn_sea(c, _):
        for j in range(GROUP):
            start = pl.multiple_of((c * GROUP + j) * LANES, LANES)
            row = sea_row[:, pl.ds(start, LANES)].astype(jnp.float32)
            cells_sea[pl.ds(start + EDGE, LANES), :] = jnp.transpose(
                jnp.broadcast_to(row, (LANES, LANES))
            )
        return 0

    lax.fori_loop(0, n // GROUP, turn_sea, 0)
    load_speed.wait()

    place = me * depth
    shift = lax.rem(place, LANES)
    row = place // LANES
    row_after = jnp.minimum(row + 1, strips - 1)
    own_speeds = jnp.where(
        lane < LANES - shift,
        pltpu.roll(jnp.broadcast_to(speed[pl.ds(row, 1), :], (EDGE, LANES)), lax.rem(LANES - shift, LANES), 1),
        pltpu.roll(jnp.broadcast_to(speed[pl.ds(row_after, 1), :], (EDGE, LANES)), lax.rem(LANES - shift, LANES), 1),
    )[0:1, :]

    load_u.wait()

    def turn_tiles(c, _):
        for j in range(GROUP):
            start = pl.multiple_of((c * GROUP + j) * LANES, LANES)
            block = u[:, pl.ds(start, LANES)]
            if depth < LANES:
                rest = jnp.zeros((LANES - depth, LANES), jnp.float32)
                block = jnp.concatenate([block, rest], axis=0)
            cells_u[pl.ds(start + EDGE, LANES), :] = jnp.transpose(block)
        return 0

    lax.fori_loop(0, n // GROUP, turn_tiles, 0)

    def make_group(group):
        for j in range(GROUP):
            tile = tile_in(group, j)
            span = pl.ds(pl.multiple_of(tile * LANES, LANES), LANES + 2 * EDGE)
            block = step_pair(cells_u[span, :], faces_of(cells_sea[span, :]), own_speeds)
            sent[tile, 0:depth, :] = jnp.transpose(block[EDGE : EDGE + LANES, :])[0:depth, :]
            edge = jnp.where(after, block[EDGE + LANES :, :], block[:EDGE, :])
            sent[tile, depth:, :] = pltpu.roll(edge, shift, 1)

    def first(dest, source, rows, count=None):
        blocks = (lambda k: k) if count is None else (lambda k: pl.ds(0, count))
        return pltpu.make_async_remote_copy(
            src_ref=sent.at[blocks(dest), 0:rows], dst_ref=got.at[blocks(source), 0:rows],
            send_sem=send_one.at[0 if rows > depth else 1], recv_sem=recv_one,
            device_id={"cell": dest}, device_id_type=MESH,
        )

    def send_groups(groups, rows):
        def body(group, _):
            make_group(group)
            for j in range(GROUP):
                dest = tile_in(group, served(j))

                @pl.when(dest != me)
                def _():
                    first(dest, me, rows).start()

            return 0

        lax.fori_loop(*groups, body, 0)

    pl.semaphore_wait(barrier, n - 1)
    send_groups((0, spread), depth + EDGE)
    send_groups((spread, 2 * spread), depth)

    got[me] = sent[me]
    start = pl.multiple_of(me * LANES, LANES)
    near_sea = [
        cells_sea[pl.ds(start + EDGE, LANES), :],
        jnp.where(after, cells_sea[pl.ds(start + EDGE + LANES, EDGE), :], cells_sea[pl.ds(start, EDGE), :]),
    ]
    near_open = faces_of(jnp.concatenate(near_sea, axis=0))

    other = lax.rem(me + 1, n)

    @pl.when(leading)
    def _():
        first(other, other, depth + EDGE, n - 1).wait_recv()

    @pl.when(jnp.logical_not(leading))
    def _():
        first(other, other, depth, n - 1).wait_recv()

    for q in range(strips):
        low, high = q * LANES, (q + 1) * LANES
        pieces = []
        for source in range(low // depth, -(-high // depth)):
            base = source * depth
            pieces.append(got[source, max(low - base, 0) : min(high - base, depth), :])
        block = jnp.transpose(jnp.concatenate(pieces, axis=0))
        state[q, :LANES, :] = block
        rounded[:LANES, low:high] = block.astype(jnp.bfloat16)

    def border(side):
        return pltpu.make_async_remote_copy(
            src_ref=state.at[:, 0:EDGE] if side else state.at[:, LANES - EDGE : LANES],
            dst_ref=beside.at[side], send_sem=send_border.at[side], recv_sem=recv_border.at[side],
            device_id={"cell": me - 1 if side else me + 1}, device_id_type=MESH,
        )

    @pl.when(leading)
    def _():
        border(0).start()

        @pl.when(me > 0)
        def _():
            border(1).start()

    @pl.when(jnp.logical_not(leading))
    def _():
        border(0).wait_recv()

        @pl.when(me < n - 1)
        def _():
            border(1).wait_recv()

        @pl.when(me == n - 1)
        def _():
            beside[1] = jnp.zeros((strips, EDGE, LANES), jnp.float32)

    height = LANES + EDGE
    for q in range(strips):
        low, high = q * LANES, (q + 1) * LANES
        edge = None
        for source in range(low // depth, -(-high // depth)):
            mine = got[source, depth:, :]
            edge = mine if edge is None else jnp.where(lane >= source * depth - low, mine, edge)
        edge = jnp.where(leading, edge, jnp.where(after, beside[1, q], beside[0, q]))
        state[q, LANES:, :] = edge
        rounded[LANES:, low:high] = jnp.concatenate([edge, none], axis=0).astype(jnp.bfloat16)

    load_lift.wait()
    lifted = dot_rows(rounded[...], lift[...])
    squared[...] = (lifted * lifted).astype(jnp.bfloat16)
    load_back.wait()

    parts = max(k for k in (4, 3, 2, 1) if strips % k == 0)
    wide = strips // parts
    for part in range(parts):
        rows = slice(part * wide * LANES, (part + 1) * wide * LANES)
        source = dot_rows(squared[...], back[rows, :])
        for k in range(wide):
            q = part * wide + k
            block = state[q] + coupling * source[:height, k * LANES : (k + 1) * LANES]
            block = step_pair(block, near_open, speed[q : q + 1, :])[:LANES, :]
            rounded[:LANES, q * LANES : (q + 1) * LANES] = block.astype(jnp.bfloat16)
            total[q * LANES : (q + 1) * LANES, :] = jnp.transpose(block)

    lifted = dot_rows(rounded[:LANES, :], lift[...])
    squared[:LANES, :] = (lifted * lifted).astype(jnp.bfloat16)

    def column(tile):
        return out_ref.at[:, pl.ds(pl.multiple_of(tile * LANES, LANES), LANES)]

    def second(dest, source):
        return pltpu.make_async_remote_copy(
            src_ref=result.at[dest], dst_ref=column(source),
            send_sem=send_two, recv_sem=recv_two,
            device_id={"cell": dest}, device_id_type=MESH,
        )

    own = pltpu.make_async_copy(result.at[me], column(me), own_sem)
    part = quarter
    comp_part = comps // 4

    def source_two(step, _):
        i = served(step)
        rows = pl.ds(pl.multiple_of(i * comp_part, comp_part), comp_part)
        source = dot_rows(back[rows, :], squared[:LANES, :])
        ended = total[rows, :] + coupling * source
        result[pl.ds(i * part, part)] = ended.reshape(part, depth, LANES)

        def send(j, _):
            dest = i * part + j

            @pl.when(dest != me)
            def _():
                second(dest, me).start()

            return 0

        lax.fori_loop(0, part, send, 0)
        return 0

    lax.fori_loop(0, 4, source_two, 0)
    own.start()

    @pl.when(leading)
    def _():
        first(other, other, depth + EDGE, half - 1).wait_send()
        first(other, other, depth, half).wait_send()
        border(0).wait_send()

        @pl.when(me > 0)
        def _():
            border(1).wait_send()

    @pl.when(jnp.logical_not(leading))
    def _():
        first(other, other, depth + EDGE, half).wait_send()
        first(other, other, depth, half - 1).wait_send()

    ended = pltpu.make_async_remote_copy(
        src_ref=result.at[0 : n - 1], dst_ref=result.at[0 : n - 1], send_sem=send_two, recv_sem=recv_two,
        device_id={"cell": other}, device_id_type=MESH,
    )
    ended.wait_send()
    ended.wait_recv()
    own.wait()


def shards(wave_energy, courant, sea_mask, lift_weight, back_weight):
    n = lax.axis_size("cell")
    groups, cells = wave_energy.shape
    modes = lift_weight.shape[0]
    depth = -(-groups // 8) * 8
    extra = depth - groups
    if extra:
        wave_energy = jnp.pad(wave_energy, ((0, extra), (0, 0)))
        courant = jnp.pad(courant.reshape(n, groups), ((0, 0), (0, extra))).reshape(-1)
        lift_weight = jnp.pad(
            lift_weight.reshape(modes, n, groups), ((0, 0), (0, 0), (0, extra))
        ).reshape(modes, n * depth)
        back_weight = jnp.pad(
            back_weight.reshape(n, groups, modes), ((0, 0), (0, extra), (0, 0))
        ).reshape(n * depth, modes)
    comps = n * depth
    strips = comps // LANES
    tall = LANES + 2 * EDGE
    buffers = [
        pltpu.VMEM((depth, cells), jnp.float32),
        pltpu.VMEM((strips, LANES), jnp.float32),
        pltpu.VMEM((1, cells), jnp.int32),
        pltpu.VMEM((n, depth + EDGE, LANES), jnp.float32),
        pltpu.VMEM((n, depth + EDGE, LANES), jnp.float32),
        pltpu.VMEM((cells + 2 * EDGE, LANES), jnp.float32),
        pltpu.VMEM((cells + 2 * EDGE, LANES), jnp.float32),
        pltpu.VMEM((strips, LANES + EDGE, LANES), jnp.float32),
        pltpu.VMEM((tall, comps), jnp.bfloat16),
        pltpu.VMEM((tall, modes), jnp.bfloat16),
        pltpu.VMEM((comps, LANES), jnp.float32),
        pltpu.VMEM((n, depth, LANES), jnp.float32),
        pltpu.VMEM((2, strips, EDGE, LANES), jnp.float32),
        pltpu.VMEM((modes, comps), jnp.bfloat16),
        pltpu.VMEM((comps, modes), jnp.bfloat16),
    ]
    held = sum(math.prod(b.shape) * jnp.dtype(b.dtype).itemsize for b in buffers)
    operands = [
        pltpu.with_memory_space_constraint(x, pltpu.HBM)
        for x in (wave_energy, courant.reshape(strips, LANES), sea_mask[None, :], lift_weight, back_weight)
    ]
    out = pl.pallas_call(
        functools.partial(kernel, n),
        out_shape=jax.ShapeDtypeStruct((depth, cells), jnp.float32),
        in_specs=[pl.BlockSpec(memory_space=pltpu.HBM)] * 5,
        out_specs=pl.BlockSpec(memory_space=pl.ANY),
        scratch_shapes=buffers
        + [
            pltpu.SemaphoreType.DMA((5,)),
            pltpu.SemaphoreType.DMA,
            pltpu.SemaphoreType.DMA((2,)),
            pltpu.SemaphoreType.DMA,
            pltpu.SemaphoreType.DMA,
            pltpu.SemaphoreType.DMA,
            pltpu.SemaphoreType.DMA((2,)),
            pltpu.SemaphoreType.DMA((2,)),
        ],
        compiler_params=pltpu.CompilerParams(
            collective_id=0, has_side_effects=True, vmem_limit_bytes=held + 4 * 1024 * 1024
        ),
    )(*operands)
    return out[:groups]


def solution(mesh):
    placed = (P(("member", "cell"), None), P(), P(), P(), P())
    return jax.shard_map(
        shards, mesh=mesh, in_specs=placed, out_specs=P(("member", "cell"), None), check_vma=False
    )
```

```python
import functools
import math

import jax
import jax.numpy as jnp
from jax import lax
from jax.experimental import pallas as pl
from jax.experimental.pallas import tpu as pltpu
from jax.sharding import PartitionSpec as P

LANES = 128
EDGE = 8
GROUP = 4
MESH = pl.DeviceIdType.MESH

SERVED = ((1, 0, 2, 3), (2, 3, 0, 1), (3, 0, 1, 2), (0, 1, 2, 3))


def pack(digits):
    return sum(digit << (2 * k) for k, digit in enumerate(digits))


coupling = 0.25


def minmod(first_term, second_term):
    low = jnp.minimum(first_term, second_term)
    high = jnp.maximum(first_term, second_term)
    return jnp.maximum(low, 0.0) + jnp.minimum(high, 0.0)


def step_pair(spectra, open_faces, speeds):
    height = spectra.shape[0]
    eastward = speeds >= 0.0
    weight = jnp.where(eastward, 0.5 * (1.0 - speeds), -0.5 * (1.0 + speeds))
    eastward = jnp.broadcast_to(eastward, spectra.shape)
    for _ in range(2):
        ahead = pltpu.roll(spectra, height - 1, 0) - spectra
        behind = pltpu.roll(ahead, 1, 0)
        carried = speeds * (spectra + weight * minmod(ahead, behind))
        flux = jnp.where(eastward, carried, pltpu.roll(carried, height - 1, 0)) * open_faces
        spectra = spectra - (flux - pltpu.roll(flux, 1, 0))
    return spectra


def faces_of(sea):
    return sea * pltpu.roll(sea, sea.shape[0] - 1, 0)


def dot_rows(a, b):
    return lax.dot_general(a, b, (((1,), (1,)), ((), ())), preferred_element_type=jnp.float32)


def kernel(
    n, u_hbm, speed_hbm, sea_hbm, lift_hbm, back_hbm, out_ref,
    u, speed, sea_row, sent, got, cells_u, cells_sea, state, rounded, squared, total, result, beside, lift, back,
    load_sem, own_sem, send_one, recv_one, send_two, recv_two, send_border, recv_border,
):
    me = lax.axis_index("cell")
    depth, cells = u_hbm.shape
    modes, comps = lift.shape
    strips = comps // LANES
    half = n // 2

    barrier = pltpu.get_barrier_semaphore()

    spread = half // GROUP
    leading = lax.rem(me, 2) == 0

    quarter = n // 4
    mine = me // quarter
    order = jnp.int32(pack(SERVED[3]))
    for k in range(3):
        order = jnp.where(mine == k, pack(SERVED[k]), order)

    def served(step):
        return jnp.right_shift(order, 2 * step) & 3

    def tile_in(group, j):
        return 2 * (j * spread + lax.rem(lax.rem(group, spread) + j, spread)) + group // spread

    load_sea = pltpu.make_async_copy(sea_hbm, sea_row, load_sem.at[0])
    load_speed = pltpu.make_async_copy(speed_hbm, speed, load_sem.at[1])
    load_u = pltpu.make_async_copy(u_hbm, u, load_sem.at[2])
    load_lift = pltpu.make_async_copy(lift_hbm, lift, load_sem.at[3])
    load_back = pltpu.make_async_copy(back_hbm, back, load_sem.at[4])
    loads = [load_sea, load_u, load_speed, load_lift, load_back]
    for load in loads:
        load.start()

    def greet(k, _):
        @pl.when(k != me)
        def _():
            pl.semaphore_signal(barrier, inc=1, device_id={"cell": k}, device_id_type=MESH)

        return 0

    lax.fori_loop(0, n, greet, 0)

    lane = lax.broadcasted_iota(jnp.int32, (EDGE, LANES), 1)
    after = lax.broadcasted_iota(jnp.int32, (EDGE, LANES), 0) < EDGE // 2

    none = jnp.zeros((EDGE, LANES), jnp.float32)
    cells_sea[0:EDGE, :] = none
    cells_sea[cells + EDGE :, :] = none
    cells_u[0:EDGE, :] = none
    cells_u[cells + EDGE :, :] = none

    load_sea.wait()

    def turn_sea(c, _):
        for j in range(GROUP):
            start = pl.multiple_of((c * GROUP + j) * LANES, LANES)
            row = sea_row[:, pl.ds(start, LANES)].astype(jnp.float32)
            cells_sea[pl.ds(start + EDGE, LANES), :] = jnp.transpose(
                jnp.broadcast_to(row, (LANES, LANES))
            )
        return 0

    lax.fori_loop(0, n // GROUP, turn_sea, 0, unroll=4)
    load_speed.wait()

    place = me * depth
    shift = lax.rem(place, LANES)
    row = place // LANES
    row_after = jnp.minimum(row + 1, strips - 1)
    own_speeds = jnp.where(
        lane < LANES - shift,
        pltpu.roll(jnp.broadcast_to(speed[pl.ds(row, 1), :], (EDGE, LANES)), lax.rem(LANES - shift, LANES), 1),
        pltpu.roll(jnp.broadcast_to(speed[pl.ds(row_after, 1), :], (EDGE, LANES)), lax.rem(LANES - shift, LANES), 1),
    )[0:1, :]

    load_u.wait()

    def turn_tiles(c, _):
        for j in range(GROUP):
            start = pl.multiple_of((c * GROUP + j) * LANES, LANES)
            block = u[:, pl.ds(start, LANES)]
            if depth < LANES:
                rest = jnp.zeros((LANES - depth, LANES), jnp.float32)
                block = jnp.concatenate([block, rest], axis=0)
            cells_u[pl.ds(start + EDGE, LANES), :] = jnp.transpose(block)
        return 0

    lax.fori_loop(0, n // GROUP, turn_tiles, 0, unroll=4)

    def make_group(group):
        for j in range(GROUP):
            tile = tile_in(group, j)
            span = pl.ds(pl.multiple_of(tile * LANES, LANES), LANES + 2 * EDGE)
            block = step_pair(cells_u[span, :], faces_of(cells_sea[span, :]), own_speeds)
            sent[tile, 0:depth, :] = jnp.transpose(block[EDGE : EDGE + LANES, :])[0:depth, :]
            edge = jnp.where(after, block[EDGE + LANES :, :], block[:EDGE, :])
            sent[tile, depth:, :] = pltpu.roll(edge, shift, 1)

    def first(dest, source, rows, count=None):
        blocks = (lambda k: k) if count is None else (lambda k: pl.ds(0, count))
        return pltpu.make_async_remote_copy(
            src_ref=sent.at[blocks(dest), 0:rows], dst_ref=got.at[blocks(source), 0:rows],
            send_sem=send_one.at[0 if rows > depth else 1], recv_sem=recv_one,
            device_id={"cell": dest}, device_id_type=MESH,
        )

    def send_group(group, rows):
        for j in range(GROUP):
            dest = tile_in(group, served(j))

            @pl.when(dest != me)
            def _():
                first(dest, me, rows).start()

    make_group(0)
    pl.semaphore_wait(barrier, n - 1)
    send_group(0, depth + EDGE)

    def even_group(group, _):
        make_group(group)
        send_group(group, depth + EDGE)
        return 0

    def odd_group(group, _):
        make_group(group)
        send_group(group, depth)
        return 0

    lax.fori_loop(1, spread, even_group, 0)
    lax.fori_loop(spread, 2 * spread, odd_group, 0)

    got[me] = sent[me]
    start = pl.multiple_of(me * LANES, LANES)
    near_sea = [
        cells_sea[pl.ds(start + EDGE, LANES), :],
        jnp.where(after, cells_sea[pl.ds(start + EDGE + LANES, EDGE), :], cells_sea[pl.ds(start, EDGE), :]),
    ]
    near_open = faces_of(jnp.concatenate(near_sea, axis=0))

    other = lax.rem(me + 1, n)

    @pl.when(leading)
    def _():
        first(other, other, depth + EDGE, n - 1).wait_recv()

    @pl.when(jnp.logical_not(leading))
    def _():
        first(other, other, depth, n - 1).wait_recv()

    for q in range(strips):
        low, high = q * LANES, (q + 1) * LANES
        pieces = []
        for source in range(low // depth, -(-high // depth)):
            base = source * depth
            pieces.append(got[source, max(low - base, 0) : min(high - base, depth), :])
        block = jnp.transpose(jnp.concatenate(pieces, axis=0))
        state[q, :LANES, :] = block
        rounded[:LANES, low:high] = block.astype(jnp.bfloat16)

    def border(side):
        return pltpu.make_async_remote_copy(
            src_ref=state.at[:, 0:EDGE] if side else state.at[:, LANES - EDGE : LANES],
            dst_ref=beside.at[side], send_sem=send_border.at[side], recv_sem=recv_border.at[side],
            device_id={"cell": me - 1 if side else me + 1}, device_id_type=MESH,
        )

    @pl.when(leading)
    def _():
        border(0).start()

        @pl.when(me > 0)
        def _():
            border(1).start()

    @pl.when(jnp.logical_not(leading))
    def _():
        border(0).wait_recv()

        @pl.when(me < n - 1)
        def _():
            border(1).wait_recv()

        @pl.when(me == n - 1)
        def _():
            beside[1] = jnp.zeros((strips, EDGE, LANES), jnp.float32)

    height = LANES + EDGE
    for q in range(strips):
        low, high = q * LANES, (q + 1) * LANES
        edge = None
        for source in range(low // depth, -(-high // depth)):
            mine = got[source, depth:, :]
            edge = mine if edge is None else jnp.where(lane >= source * depth - low, mine, edge)
        edge = jnp.where(leading, edge, jnp.where(after, beside[1, q], beside[0, q]))
        state[q, LANES:, :] = edge
        rounded[LANES:, low:high] = jnp.concatenate([edge, none], axis=0).astype(jnp.bfloat16)

    load_lift.wait()
    lifted = dot_rows(rounded[...], lift[...])
    squared[...] = (lifted * lifted).astype(jnp.bfloat16)
    load_back.wait()

    parts = max(k for k in (4, 3, 2, 1) if strips % k == 0)
    wide = strips // parts
    for part in range(parts):
        rows = slice(part * wide * LANES, (part + 1) * wide * LANES)
        source = dot_rows(squared[...], back[rows, :])
        for k in range(wide):
            q = part * wide + k
            block = state[q] + coupling * source[:height, k * LANES : (k + 1) * LANES]
            block = step_pair(block, near_open, speed[q : q + 1, :])[:LANES, :]
            rounded[:LANES, q * LANES : (q + 1) * LANES] = block.astype(jnp.bfloat16)
            total[q * LANES : (q + 1) * LANES, :] = jnp.transpose(block)

    lifted = dot_rows(rounded[:LANES, :], lift[...])
    squared[:LANES, :] = (lifted * lifted).astype(jnp.bfloat16)

    def column(tile):
        return out_ref.at[:, pl.ds(pl.multiple_of(tile * LANES, LANES), LANES)]

    def second(dest, source):
        return pltpu.make_async_remote_copy(
            src_ref=result.at[dest], dst_ref=column(source),
            send_sem=send_two, recv_sem=recv_two,
            device_id={"cell": dest}, device_id_type=MESH,
        )

    own = pltpu.make_async_copy(result.at[me], column(me), own_sem)
    part = quarter
    comp_part = comps // 4

    def source_two(step, _):
        i = served(step)
        rows = pl.ds(pl.multiple_of(i * comp_part, comp_part), comp_part)
        source = dot_rows(back[rows, :], squared[:LANES, :])
        ended = total[rows, :] + coupling * source
        result[pl.ds(i * part, part)] = ended.reshape(part, depth, LANES)

        def send(j, _):
            dest = i * part + j

            @pl.when(dest != me)
            def _():
                second(dest, me).start()

            return 0

        lax.fori_loop(0, part, send, 0)
        return 0

    lax.fori_loop(0, 4, source_two, 0)
    own.start()

    @pl.when(leading)
    def _():
        first(other, other, depth + EDGE, half - 1).wait_send()
        first(other, other, depth, half).wait_send()
        border(0).wait_send()

        @pl.when(me > 0)
        def _():
            border(1).wait_send()

    @pl.when(jnp.logical_not(leading))
    def _():
        first(other, other, depth + EDGE, half).wait_send()
        first(other, other, depth, half - 1).wait_send()

    ended = pltpu.make_async_remote_copy(
        src_ref=result.at[0 : n - 1], dst_ref=result.at[0 : n - 1], send_sem=send_two, recv_sem=recv_two,
        device_id={"cell": other}, device_id_type=MESH,
    )
    ended.wait_send()
    ended.wait_recv()
    own.wait()


def shards(wave_energy, courant, sea_mask, lift_weight, back_weight):
    n = lax.axis_size("cell")
    groups, cells = wave_energy.shape
    modes = lift_weight.shape[0]
    depth = -(-groups // 8) * 8
    extra = depth - groups
    if extra:
        wave_energy = jnp.pad(wave_energy, ((0, extra), (0, 0)))
        courant = jnp.pad(courant.reshape(n, groups), ((0, 0), (0, extra))).reshape(-1)
        lift_weight = jnp.pad(
            lift_weight.reshape(modes, n, groups), ((0, 0), (0, 0), (0, extra))
        ).reshape(modes, n * depth)
        back_weight = jnp.pad(
            back_weight.reshape(n, groups, modes), ((0, 0), (0, extra), (0, 0))
        ).reshape(n * depth, modes)
    comps = n * depth
    strips = comps // LANES
    tall = LANES + 2 * EDGE
    buffers = [
        pltpu.VMEM((depth, cells), jnp.float32),
        pltpu.VMEM((strips, LANES), jnp.float32),
        pltpu.VMEM((1, cells), jnp.int32),
        pltpu.VMEM((n, depth + EDGE, LANES), jnp.float32),
        pltpu.VMEM((n, depth + EDGE, LANES), jnp.float32),
        pltpu.VMEM((cells + 2 * EDGE, LANES), jnp.float32),
        pltpu.VMEM((cells + 2 * EDGE, LANES), jnp.float32),
        pltpu.VMEM((strips, LANES + EDGE, LANES), jnp.float32),
        pltpu.VMEM((tall, comps), jnp.bfloat16),
        pltpu.VMEM((tall, modes), jnp.bfloat16),
        pltpu.VMEM((comps, LANES), jnp.float32),
        pltpu.VMEM((n, depth, LANES), jnp.float32),
        pltpu.VMEM((2, strips, EDGE, LANES), jnp.float32),
        pltpu.VMEM((modes, comps), jnp.bfloat16),
        pltpu.VMEM((comps, modes), jnp.bfloat16),
    ]
    held = sum(math.prod(b.shape) * jnp.dtype(b.dtype).itemsize for b in buffers)
    operands = [
        pltpu.with_memory_space_constraint(x, pltpu.HBM)
        for x in (wave_energy, courant.reshape(strips, LANES), sea_mask[None, :], lift_weight, back_weight)
    ]
    out = pl.pallas_call(
        functools.partial(kernel, n),
        out_shape=jax.ShapeDtypeStruct((depth, cells), jnp.float32),
        in_specs=[pl.BlockSpec(memory_space=pltpu.HBM)] * 5,
        out_specs=pl.BlockSpec(memory_space=pl.ANY),
        scratch_shapes=buffers
        + [
            pltpu.SemaphoreType.DMA((5,)),
            pltpu.SemaphoreType.DMA,
            pltpu.SemaphoreType.DMA((2,)),
            pltpu.SemaphoreType.DMA,
            pltpu.SemaphoreType.DMA,
            pltpu.SemaphoreType.DMA,
            pltpu.SemaphoreType.DMA((2,)),
            pltpu.SemaphoreType.DMA((2,)),
        ],
        compiler_params=pltpu.CompilerParams(
            collective_id=0, has_side_effects=True, vmem_limit_bytes=held + 4 * 1024 * 1024
        ),
    )(*operands)
    return out[:groups]


def solution(mesh):
    placed = (P(("member", "cell"), None), P(), P(), P(), P())
    return jax.shard_map(
        shards, mesh=mesh, in_specs=placed, out_specs=P(("member", "cell"), None), check_vma=False
    )
```

```python
import functools
import math

import jax
import jax.numpy as jnp
from jax import lax
from jax.experimental import pallas as pl
from jax.experimental.pallas import tpu as pltpu
from jax.sharding import PartitionSpec as P

LANES = 128
EDGE = 8
GROUP = 4
MESH = pl.DeviceIdType.MESH

SERVED = ((1, 0, 2, 3), (2, 3, 0, 1), (3, 0, 1, 2), (0, 1, 2, 3))


def pack(digits):
    return sum(digit << (2 * k) for k, digit in enumerate(digits))


coupling = 0.25


def minmod(first_term, second_term):
    low = jnp.minimum(first_term, second_term)
    high = jnp.maximum(first_term, second_term)
    return jnp.maximum(low, 0.0) + jnp.minimum(high, 0.0)


def step_pair(spectra, open_faces, speeds):
    height = spectra.shape[0]
    eastward = speeds >= 0.0
    weight = jnp.where(eastward, 0.5 * (1.0 - speeds), -0.5 * (1.0 + speeds))
    eastward = jnp.broadcast_to(eastward, spectra.shape)
    for _ in range(2):
        ahead = pltpu.roll(spectra, height - 1, 0) - spectra
        behind = pltpu.roll(ahead, 1, 0)
        carried = speeds * (spectra + weight * minmod(ahead, behind))
        flux = jnp.where(eastward, carried, pltpu.roll(carried, height - 1, 0)) * open_faces
        spectra = spectra - (flux - pltpu.roll(flux, 1, 0))
    return spectra


def faces_of(sea):
    return sea * pltpu.roll(sea, sea.shape[0] - 1, 0)


def dot_rows(a, b):
    return lax.dot_general(a, b, (((1,), (1,)), ((), ())), preferred_element_type=jnp.float32)


def kernel(
    n, u_hbm, speed_hbm, sea_hbm, lift_hbm, back_hbm, out_ref,
    u, speed, sea_row, sent, got, cells_u, cells_sea, state, rounded, squared, total, result, beside, lift, back,
    load_sem, own_sem, send_one, recv_one, send_two, recv_two, send_border, recv_border,
):
    me = lax.axis_index("cell")
    depth, cells = u_hbm.shape
    modes, comps = lift.shape
    strips = comps // LANES
    half = n // 2

    barrier = pltpu.get_barrier_semaphore()

    spread = half // GROUP
    leading = lax.rem(me, 2) == 0

    quarter = n // 4
    mine = me // quarter
    order = jnp.int32(pack(SERVED[3]))
    for k in range(3):
        order = jnp.where(mine == k, pack(SERVED[k]), order)

    def served(step):
        return jnp.right_shift(order, 2 * step) & 3

    def tile_in(group, j):
        return 2 * (j * spread + lax.rem(lax.rem(group, spread) + j, spread)) + group // spread

    load_sea = pltpu.make_async_copy(sea_hbm, sea_row, load_sem.at[0])
    load_speed = pltpu.make_async_copy(speed_hbm, speed, load_sem.at[1])
    load_u = pltpu.make_async_copy(u_hbm, u, load_sem.at[2])
    load_lift = pltpu.make_async_copy(lift_hbm, lift, load_sem.at[3])
    load_back = pltpu.make_async_copy(back_hbm, back, load_sem.at[4])
    loads = [load_sea, load_u, load_speed, load_lift, load_back]
    for load in loads:
        load.start()

    def greet(k, _):
        @pl.when(k != me)
        def _():
            pl.semaphore_signal(barrier, inc=1, device_id={"cell": k}, device_id_type=MESH)

        return 0

    lax.fori_loop(0, n, greet, 0)

    lane = lax.broadcasted_iota(jnp.int32, (EDGE, LANES), 1)
    after = lax.broadcasted_iota(jnp.int32, (EDGE, LANES), 0) < EDGE // 2

    none = jnp.zeros((EDGE, LANES), jnp.float32)
    cells_sea[0:EDGE, :] = none
    cells_sea[cells + EDGE :, :] = none
    cells_u[0:EDGE, :] = none
    cells_u[cells + EDGE :, :] = none

    load_sea.wait()

    def turn_sea(c, _):
        for j in range(GROUP):
            start = pl.multiple_of((c * GROUP + j) * LANES, LANES)
            row = sea_row[:, pl.ds(start, LANES)].astype(jnp.float32)
            cells_sea[pl.ds(start + EDGE, LANES), :] = jnp.transpose(
                jnp.broadcast_to(row, (LANES, LANES))
            )
        return 0

    lax.fori_loop(0, n // GROUP, turn_sea, 0, unroll=4)
    load_speed.wait()

    place = me * depth
    shift = lax.rem(place, LANES)
    row = place // LANES
    row_after = jnp.minimum(row + 1, strips - 1)
    own_speeds = jnp.where(
        lane < LANES - shift,
        pltpu.roll(jnp.broadcast_to(speed[pl.ds(row, 1), :], (EDGE, LANES)), lax.rem(LANES - shift, LANES), 1),
        pltpu.roll(jnp.broadcast_to(speed[pl.ds(row_after, 1), :], (EDGE, LANES)), lax.rem(LANES - shift, LANES), 1),
    )[0:1, :]

    load_u.wait()

    def turn_tiles(c, _):
        for j in range(GROUP):
            start = pl.multiple_of((c * GROUP + j) * LANES, LANES)
            block = u[:, pl.ds(start, LANES)]
            if depth < LANES:
                rest = jnp.zeros((LANES - depth, LANES), jnp.float32)
                block = jnp.concatenate([block, rest], axis=0)
            cells_u[pl.ds(start + EDGE, LANES), :] = jnp.transpose(block)
        return 0

    lax.fori_loop(0, n // GROUP, turn_tiles, 0, unroll=4)

    over = max(2 * depth - LANES, 0)
    extra = EDGE // 2 + (over > 0)
    row_of = lax.broadcasted_iota(jnp.int32, (EDGE, LANES), 0)

    def turn(x, down, right):
        x = pltpu.roll(x, down % EDGE, 0) if down % EDGE else x
        return pltpu.roll(x, right % LANES, 1) if right % LANES else x

    def pack_edge(edge):
        before = turn(edge, EDGE // 2, depth)
        packed = jnp.where(lane < depth, edge, before)
        if over:
            rest = turn(before, EDGE // 2, 0)
            for r in range(1, EDGE // 2):
                rest = jnp.where(lane >= over * r, turn(before, EDGE // 2 - r, over * r), rest)
            packed = jnp.where(after, packed, rest)
        return packed

    def unpack_edge(packed, right):
        before = turn(packed, EDGE // 2, -depth)
        if over:
            rest = turn(packed, 0, -depth)
            for r in range(1, EDGE // 2):
                rest = jnp.where(row_of == EDGE // 2 + r, turn(packed, r, -depth - over * r), rest)
            before = jnp.where(lane < LANES - depth, before, rest)
        return turn(jnp.where(after, packed, before), 0, right)

    def make_group(group):
        for j in range(GROUP):
            tile = tile_in(group, j)
            span = pl.ds(pl.multiple_of(tile * LANES, LANES), LANES + 2 * EDGE)
            block = step_pair(cells_u[span, :], faces_of(cells_sea[span, :]), own_speeds)
            sent[tile, 0:depth, :] = jnp.transpose(block[EDGE : EDGE + LANES, :])[0:depth, :]
            edge = jnp.where(after, block[EDGE + LANES :, :], block[:EDGE, :])
            sent[tile, depth:, :] = pack_edge(edge)

    def first(dest, source, rows, count=None):
        blocks = (lambda k: k) if count is None else (lambda k: pl.ds(0, count))
        return pltpu.make_async_remote_copy(
            src_ref=sent.at[blocks(dest), 0:rows], dst_ref=got.at[blocks(source), 0:rows],
            send_sem=send_one.at[0 if rows > depth else 1], recv_sem=recv_one,
            device_id={"cell": dest}, device_id_type=MESH,
        )

    def send_group(group, rows):
        for j in range(GROUP):
            dest = tile_in(group, j)

            @pl.when(dest != me)
            def _():
                first(dest, me, rows).start()

    make_group(0)
    pl.semaphore_wait(barrier, n - 1)
    send_group(0, depth + extra)

    def even_group(group, _):
        make_group(group)
        send_group(group, depth + extra)
        return 0

    def odd_group(group, _):
        make_group(group)
        send_group(group, depth)
        return 0

    lax.fori_loop(1, spread, even_group, 0)
    lax.fori_loop(spread, 2 * spread, odd_group, 0)

    got[me] = sent[me]
    start = pl.multiple_of(me * LANES, LANES)
    near_sea = [
        cells_sea[pl.ds(start + EDGE, LANES), :],
        jnp.where(after, cells_sea[pl.ds(start + EDGE + LANES, EDGE), :], cells_sea[pl.ds(start, EDGE), :]),
    ]
    near_open = faces_of(jnp.concatenate(near_sea, axis=0))

    other = lax.rem(me + 1, n)

    @pl.when(leading)
    def _():
        first(other, other, depth + extra, n - 1).wait_recv()

    @pl.when(jnp.logical_not(leading))
    def _():
        first(other, other, depth, n - 1).wait_recv()

    for q in range(strips):
        low, high = q * LANES, (q + 1) * LANES
        pieces = []
        for source in range(low // depth, -(-high // depth)):
            base = source * depth
            pieces.append(got[source, max(low - base, 0) : min(high - base, depth), :])
        block = jnp.transpose(jnp.concatenate(pieces, axis=0))
        state[q, :LANES, :] = block
        rounded[:LANES, low:high] = block.astype(jnp.bfloat16)

    def border(side):
        return pltpu.make_async_remote_copy(
            src_ref=state.at[:, 0:EDGE] if side else state.at[:, LANES - EDGE : LANES],
            dst_ref=beside.at[side], send_sem=send_border.at[side], recv_sem=recv_border.at[side],
            device_id={"cell": me - 1 if side else me + 1}, device_id_type=MESH,
        )

    @pl.when(leading)
    def _():
        border(0).start()

        @pl.when(me > 0)
        def _():
            border(1).start()

    @pl.when(jnp.logical_not(leading))
    def _():
        border(0).wait_recv()

        @pl.when(me < n - 1)
        def _():
            border(1).wait_recv()

        @pl.when(me == n - 1)
        def _():
            beside[1] = jnp.zeros((strips, EDGE, LANES), jnp.float32)

    height = LANES + EDGE
    for q in range(strips):
        low, high = q * LANES, (q + 1) * LANES
        edge = None
        for source in range(low // depth, -(-high // depth)):
            mine = unpack_edge(got[source, depth:, :], source * depth)
            edge = mine if edge is None else jnp.where(lane >= source * depth - low, mine, edge)
        edge = jnp.where(leading, edge, jnp.where(after, beside[1, q], beside[0, q]))
        state[q, LANES:, :] = edge
        rounded[LANES:, low:high] = jnp.concatenate([edge, none], axis=0).astype(jnp.bfloat16)

    load_lift.wait()
    lifted = dot_rows(rounded[...], lift[...])
    squared[...] = (lifted * lifted).astype(jnp.bfloat16)
    load_back.wait()

    parts = max(k for k in (4, 3, 2, 1) if strips % k == 0)
    wide = strips // parts
    for part in range(parts):
        rows = slice(part * wide * LANES, (part + 1) * wide * LANES)
        source = dot_rows(squared[...], back[rows, :])
        for k in range(wide):
            q = part * wide + k
            block = state[q] + coupling * source[:height, k * LANES : (k + 1) * LANES]
            block = step_pair(block, near_open, speed[q : q + 1, :])[:LANES, :]
            rounded[:LANES, q * LANES : (q + 1) * LANES] = block.astype(jnp.bfloat16)
            total[q * LANES : (q + 1) * LANES, :] = jnp.transpose(block)

    lifted = dot_rows(rounded[:LANES, :], lift[...])
    squared[:LANES, :] = (lifted * lifted).astype(jnp.bfloat16)

    def column(tile):
        return out_ref.at[:, pl.ds(pl.multiple_of(tile * LANES, LANES), LANES)]

    def second(dest, source):
        return pltpu.make_async_remote_copy(
            src_ref=result.at[dest], dst_ref=column(source),
            send_sem=send_two, recv_sem=recv_two,
            device_id={"cell": dest}, device_id_type=MESH,
        )

    own = pltpu.make_async_copy(result.at[me], column(me), own_sem)
    part = quarter
    comp_part = comps // 4

    def source_two(step, _):
        i = served(step)
        rows = pl.ds(pl.multiple_of(i * comp_part, comp_part), comp_part)
        source = dot_rows(back[rows, :], squared[:LANES, :])
        ended = total[rows, :] + coupling * source
        result[pl.ds(i * part, part)] = ended.reshape(part, depth, LANES)

        def send(j, _):
            dest = i * part + j

            @pl.when(dest != me)
            def _():
                second(dest, me).start()

            return 0

        lax.fori_loop(0, part, send, 0)
        return 0

    lax.fori_loop(0, 4, source_two, 0)
    own.start()

    @pl.when(leading)
    def _():
        first(other, other, depth + extra, half - 1).wait_send()
        first(other, other, depth, half).wait_send()
        border(0).wait_send()

        @pl.when(me > 0)
        def _():
            border(1).wait_send()

    @pl.when(jnp.logical_not(leading))
    def _():
        first(other, other, depth + extra, half).wait_send()
        first(other, other, depth, half - 1).wait_send()

    ended = pltpu.make_async_remote_copy(
        src_ref=result.at[0 : n - 1], dst_ref=result.at[0 : n - 1], send_sem=send_two, recv_sem=recv_two,
        device_id={"cell": other}, device_id_type=MESH,
    )
    ended.wait_send()
    ended.wait_recv()
    own.wait()


def shards(wave_energy, courant, sea_mask, lift_weight, back_weight):
    n = lax.axis_size("cell")
    groups, cells = wave_energy.shape
    modes = lift_weight.shape[0]
    depth = -(-groups // 8) * 8
    extra = depth - groups
    if extra:
        wave_energy = jnp.pad(wave_energy, ((0, extra), (0, 0)))
        courant = jnp.pad(courant.reshape(n, groups), ((0, 0), (0, extra))).reshape(-1)
        lift_weight = jnp.pad(
            lift_weight.reshape(modes, n, groups), ((0, 0), (0, 0), (0, extra))
        ).reshape(modes, n * depth)
        back_weight = jnp.pad(
            back_weight.reshape(n, groups, modes), ((0, 0), (0, extra), (0, 0))
        ).reshape(n * depth, modes)
    comps = n * depth
    strips = comps // LANES
    tall = LANES + 2 * EDGE
    buffers = [
        pltpu.VMEM((depth, cells), jnp.float32),
        pltpu.VMEM((strips, LANES), jnp.float32),
        pltpu.VMEM((1, cells), jnp.int32),
        pltpu.VMEM((n, depth + EDGE, LANES), jnp.float32),
        pltpu.VMEM((n, depth + EDGE, LANES), jnp.float32),
        pltpu.VMEM((cells + 2 * EDGE, LANES), jnp.float32),
        pltpu.VMEM((cells + 2 * EDGE, LANES), jnp.float32),
        pltpu.VMEM((strips, LANES + EDGE, LANES), jnp.float32),
        pltpu.VMEM((tall, comps), jnp.bfloat16),
        pltpu.VMEM((tall, modes), jnp.bfloat16),
        pltpu.VMEM((comps, LANES), jnp.float32),
        pltpu.VMEM((n, depth, LANES), jnp.float32),
        pltpu.VMEM((2, strips, EDGE, LANES), jnp.float32),
        pltpu.VMEM((modes, comps), jnp.bfloat16),
        pltpu.VMEM((comps, modes), jnp.bfloat16),
    ]
    held = sum(math.prod(b.shape) * jnp.dtype(b.dtype).itemsize for b in buffers)
    operands = [
        pltpu.with_memory_space_constraint(x, pltpu.HBM)
        for x in (wave_energy, courant.reshape(strips, LANES), sea_mask[None, :], lift_weight, back_weight)
    ]
    out = pl.pallas_call(
        functools.partial(kernel, n),
        out_shape=jax.ShapeDtypeStruct((depth, cells), jnp.float32),
        in_specs=[pl.BlockSpec(memory_space=pltpu.HBM)] * 5,
        out_specs=pl.BlockSpec(memory_space=pl.ANY),
        scratch_shapes=buffers
        + [
            pltpu.SemaphoreType.DMA((5,)),
            pltpu.SemaphoreType.DMA,
            pltpu.SemaphoreType.DMA((2,)),
            pltpu.SemaphoreType.DMA,
            pltpu.SemaphoreType.DMA,
            pltpu.SemaphoreType.DMA,
            pltpu.SemaphoreType.DMA((2,)),
            pltpu.SemaphoreType.DMA((2,)),
        ],
        compiler_params=pltpu.CompilerParams(
            collective_id=0, has_side_effects=True, vmem_limit_bytes=held + 4 * 1024 * 1024
        ),
    )(*operands)
    return out[:groups]


def solution(mesh):
    placed = (P(("member", "cell"), None), P(), P(), P(), P())
    return jax.shard_map(
        shards, mesh=mesh, in_specs=placed, out_specs=P(("member", "cell"), None), check_vma=False
    )
```

```python
import functools
import math

import jax
import jax.numpy as jnp
from jax import lax
from jax.experimental import pallas as pl
from jax.experimental.pallas import tpu as pltpu
from jax.sharding import PartitionSpec as P

LANES = 128
EDGE = 8
GROUP = 4
MESH = pl.DeviceIdType.MESH

SERVED = ((1, 0, 2, 3), (2, 3, 0, 1), (3, 0, 1, 2), (0, 1, 2, 3))


def pack(digits):
    return sum(digit << (2 * k) for k, digit in enumerate(digits))


coupling = 0.25


def minmod(first_term, second_term):
    low = jnp.minimum(first_term, second_term)
    high = jnp.maximum(first_term, second_term)
    return jnp.maximum(low, 0.0) + jnp.minimum(high, 0.0)


def step_pair(spectra, open_faces, speeds):
    height = spectra.shape[0]
    eastward = speeds >= 0.0
    weight = jnp.where(eastward, 0.5 * (1.0 - speeds), -0.5 * (1.0 + speeds))
    eastward = jnp.broadcast_to(eastward, spectra.shape)
    for _ in range(2):
        ahead = pltpu.roll(spectra, height - 1, 0) - spectra
        behind = pltpu.roll(ahead, 1, 0)
        carried = speeds * (spectra + weight * minmod(ahead, behind))
        flux = jnp.where(eastward, carried, pltpu.roll(carried, height - 1, 0)) * open_faces
        spectra = spectra - (flux - pltpu.roll(flux, 1, 0))
    return spectra


def faces_of(sea):
    return sea * pltpu.roll(sea, sea.shape[0] - 1, 0)


def dot_rows(a, b):
    return lax.dot_general(a, b, (((1,), (1,)), ((), ())), preferred_element_type=jnp.float32)


def kernel(
    n, u_hbm, speed_hbm, sea_hbm, lift_hbm, back_hbm, out_ref,
    u, speed, sea_row, sent, got, cells_u, cells_sea, state, rounded, squared, total, result, beside, lift, back,
    load_sem, own_sem, send_one, recv_one, send_two, recv_two, send_border, recv_border,
):
    me = lax.axis_index("cell")
    depth, cells = u_hbm.shape
    modes, comps = lift.shape
    strips = comps // LANES
    half = n // 2

    barrier = pltpu.get_barrier_semaphore()

    spread = half // GROUP
    leading = lax.rem(me, 2) == 0

    quarter = n // 4
    mine = me // quarter
    order = jnp.int32(pack(SERVED[3]))
    for k in range(3):
        order = jnp.where(mine == k, pack(SERVED[k]), order)

    def served(step):
        return jnp.right_shift(order, 2 * step) & 3

    def tile_in(group, j):
        return 2 * (j * spread + lax.rem(lax.rem(group, spread) + j, spread)) + group // spread

    load_sea = pltpu.make_async_copy(sea_hbm, sea_row, load_sem.at[0])
    load_speed = pltpu.make_async_copy(speed_hbm, speed, load_sem.at[1])
    load_u = pltpu.make_async_copy(u_hbm, u, load_sem.at[2])
    load_lift = pltpu.make_async_copy(lift_hbm, lift, load_sem.at[3])
    load_back = pltpu.make_async_copy(back_hbm, back, load_sem.at[4])
    loads = [load_sea, load_u, load_speed, load_lift, load_back]
    for load in loads:
        load.start()

    def greet(k, _):
        @pl.when(k != me)
        def _():
            pl.semaphore_signal(barrier, inc=1, device_id={"cell": k}, device_id_type=MESH)

        return 0

    lax.fori_loop(0, n, greet, 0)

    lane = lax.broadcasted_iota(jnp.int32, (EDGE, LANES), 1)
    after = lax.broadcasted_iota(jnp.int32, (EDGE, LANES), 0) < EDGE // 2

    none = jnp.zeros((EDGE, LANES), jnp.float32)
    cells_sea[0:EDGE, :] = none
    cells_sea[cells + EDGE :, :] = none
    cells_u[0:EDGE, :] = none
    cells_u[cells + EDGE :, :] = none

    load_sea.wait()

    def turn_sea(c, _):
        for j in range(GROUP):
            start = pl.multiple_of((c * GROUP + j) * LANES, LANES)
            row = sea_row[:, pl.ds(start, LANES)].astype(jnp.float32)
            cells_sea[pl.ds(start + EDGE, LANES), :] = jnp.transpose(
                jnp.broadcast_to(row, (LANES, LANES))
            )
        return 0

    lax.fori_loop(0, n // GROUP, turn_sea, 0, unroll=4)
    load_speed.wait()

    place = me * depth
    shift = lax.rem(place, LANES)
    row = place // LANES
    row_after = jnp.minimum(row + 1, strips - 1)
    own_speeds = jnp.where(
        lane < LANES - shift,
        pltpu.roll(jnp.broadcast_to(speed[pl.ds(row, 1), :], (EDGE, LANES)), lax.rem(LANES - shift, LANES), 1),
        pltpu.roll(jnp.broadcast_to(speed[pl.ds(row_after, 1), :], (EDGE, LANES)), lax.rem(LANES - shift, LANES), 1),
    )[0:1, :]

    load_u.wait()

    def turn_tiles(c, _):
        for j in range(GROUP):
            start = pl.multiple_of((c * GROUP + j) * LANES, LANES)
            block = u[:, pl.ds(start, LANES)]
            if depth < LANES:
                rest = jnp.zeros((LANES - depth, LANES), jnp.float32)
                block = jnp.concatenate([block, rest], axis=0)
            cells_u[pl.ds(start + EDGE, LANES), :] = jnp.transpose(block)
        return 0

    lax.fori_loop(0, n // GROUP, turn_tiles, 0, unroll=4)

    over = max(2 * depth - LANES, 0)
    extra = EDGE // 2 + (over > 0)
    row_of = lax.broadcasted_iota(jnp.int32, (EDGE, LANES), 0)

    def turn(x, down, right):
        x = pltpu.roll(x, down % EDGE, 0) if down % EDGE else x
        return pltpu.roll(x, right % LANES, 1) if right % LANES else x

    def pack_edge(edge):
        before = turn(edge, EDGE // 2, depth)
        packed = jnp.where(lane < depth, edge, before)
        if over:
            rest = turn(before, EDGE // 2, 0)
            for r in range(1, EDGE // 2):
                rest = jnp.where(lane >= over * r, turn(before, EDGE // 2 - r, over * r), rest)
            packed = jnp.where(after, packed, rest)
        return packed

    def unpack_edge(packed, right):
        before = turn(packed, EDGE // 2, -depth)
        if over:
            rest = turn(packed, 0, -depth)
            for r in range(1, EDGE // 2):
                rest = jnp.where(row_of == EDGE // 2 + r, turn(packed, r, -depth - over * r), rest)
            before = jnp.where(lane < LANES - depth, before, rest)
        return turn(jnp.where(after, packed, before), 0, right)

    def make_group(group, halo):
        for j in range(GROUP):
            tile = tile_in(group, j)
            span = pl.ds(pl.multiple_of(tile * LANES, LANES), LANES + 2 * EDGE)
            block = step_pair(cells_u[span, :], faces_of(cells_sea[span, :]), own_speeds)
            sent[tile, 0:depth, :] = jnp.transpose(block[EDGE : EDGE + LANES, :])[0:depth, :]
            if halo:
                edge = jnp.where(after, block[EDGE + LANES :, :], block[:EDGE, :])
                sent[tile, depth:, :] = pack_edge(edge)

    def first(dest, source, rows, count=None):
        blocks = (lambda k: k) if count is None else (lambda k: pl.ds(0, count))
        return pltpu.make_async_remote_copy(
            src_ref=sent.at[blocks(dest), 0:rows], dst_ref=got.at[blocks(source), 0:rows],
            send_sem=send_one.at[0 if rows > depth else 1], recv_sem=recv_one,
            device_id={"cell": dest}, device_id_type=MESH,
        )

    def send_group(group, rows):
        for j in range(GROUP):
            dest = tile_in(group, j)

            @pl.when(dest != me)
            def _():
                first(dest, me, rows).start()

    make_group(0, True)
    pl.semaphore_wait(barrier, n - 1)
    send_group(0, depth + extra)

    def even_group(group, _):
        make_group(group, True)
        send_group(group, depth + extra)
        return 0

    def odd_group(group, _):
        make_group(group, False)
        send_group(group, depth)
        return 0

    lax.fori_loop(1, spread, even_group, 0)
    lax.fori_loop(spread, 2 * spread, odd_group, 0)

    got[me] = sent[me]
    start = pl.multiple_of(me * LANES, LANES)
    near_sea = [
        cells_sea[pl.ds(start + EDGE, LANES), :],
        jnp.where(after, cells_sea[pl.ds(start + EDGE + LANES, EDGE), :], cells_sea[pl.ds(start, EDGE), :]),
    ]
    near_open = faces_of(jnp.concatenate(near_sea, axis=0))

    other = lax.rem(me + 1, n)

    @pl.when(leading)
    def _():
        first(other, other, depth + extra, n - 1).wait_recv()

    @pl.when(jnp.logical_not(leading))
    def _():
        first(other, other, depth, n - 1).wait_recv()

    for q in range(strips):
        low, high = q * LANES, (q + 1) * LANES
        pieces = []
        for source in range(low // depth, -(-high // depth)):
            base = source * depth
            pieces.append(got[source, max(low - base, 0) : min(high - base, depth), :])
        block = jnp.transpose(jnp.concatenate(pieces, axis=0))
        state[q, :LANES, :] = block
        rounded[:LANES, low:high] = block.astype(jnp.bfloat16)

    @pl.when(leading)
    def _():
        for source in range(n):
            got[source, depth:, :] = unpack_edge(got[source, depth:, :], source * depth)

    def border(side):
        return pltpu.make_async_remote_copy(
            src_ref=state.at[:, 0:EDGE] if side else state.at[:, LANES - EDGE : LANES],
            dst_ref=beside.at[side], send_sem=send_border.at[side], recv_sem=recv_border.at[side],
            device_id={"cell": me - 1 if side else me + 1}, device_id_type=MESH,
        )

    @pl.when(leading)
    def _():
        border(0).start()

        @pl.when(me > 0)
        def _():
            border(1).start()

    @pl.when(jnp.logical_not(leading))
    def _():
        border(0).wait_recv()

        @pl.when(me < n - 1)
        def _():
            border(1).wait_recv()

        @pl.when(me == n - 1)
        def _():
            beside[1] = jnp.zeros((strips, EDGE, LANES), jnp.float32)

    height = LANES + EDGE
    for q in range(strips):
        low, high = q * LANES, (q + 1) * LANES
        edge = None
        for source in range(low // depth, -(-high // depth)):
            mine = got[source, depth:, :]
            edge = mine if edge is None else jnp.where(lane >= source * depth - low, mine, edge)
        edge = jnp.where(leading, edge, jnp.where(after, beside[1, q], beside[0, q]))
        state[q, LANES:, :] = edge
        rounded[LANES:, low:high] = jnp.concatenate([edge, none], axis=0).astype(jnp.bfloat16)

    load_lift.wait()
    lifted = dot_rows(rounded[...], lift[...])
    squared[...] = (lifted * lifted).astype(jnp.bfloat16)
    load_back.wait()

    parts = max(k for k in (4, 3, 2, 1) if strips % k == 0)
    wide = strips // parts
    for part in range(parts):
        rows = slice(part * wide * LANES, (part + 1) * wide * LANES)
        source = dot_rows(squared[...], back[rows, :])
        for k in range(wide):
            q = part * wide + k
            block = state[q] + coupling * source[:height, k * LANES : (k + 1) * LANES]
            block = step_pair(block, near_open, speed[q : q + 1, :])[:LANES, :]
            rounded[:LANES, q * LANES : (q + 1) * LANES] = block.astype(jnp.bfloat16)
            total[q * LANES : (q + 1) * LANES, :] = jnp.transpose(block)

    lifted = dot_rows(rounded[:LANES, :], lift[...])
    squared[:LANES, :] = (lifted * lifted).astype(jnp.bfloat16)

    def column(tile):
        return out_ref.at[:, pl.ds(pl.multiple_of(tile * LANES, LANES), LANES)]

    def second(dest, source):
        return pltpu.make_async_remote_copy(
            src_ref=result.at[dest], dst_ref=column(source),
            send_sem=send_two, recv_sem=recv_two,
            device_id={"cell": dest}, device_id_type=MESH,
        )

    own = pltpu.make_async_copy(result.at[me], column(me), own_sem)
    part = quarter
    comp_part = comps // 4

    def source_two(step, _):
        i = served(step)
        rows = pl.ds(pl.multiple_of(i * comp_part, comp_part), comp_part)
        source = dot_rows(back[rows, :], squared[:LANES, :])
        ended = total[rows, :] + coupling * source
        result[pl.ds(i * part, part)] = ended.reshape(part, depth, LANES)

        def send(j, _):
            dest = i * part + j

            @pl.when(dest != me)
            def _():
                second(dest, me).start()

            return 0

        lax.fori_loop(0, part, send, 0)
        return 0

    lax.fori_loop(0, 4, source_two, 0)
    own.start()

    @pl.when(leading)
    def _():
        first(other, other, depth + extra, half - 1).wait_send()
        first(other, other, depth, half).wait_send()
        border(0).wait_send()

        @pl.when(me > 0)
        def _():
            border(1).wait_send()

    @pl.when(jnp.logical_not(leading))
    def _():
        first(other, other, depth + extra, half).wait_send()
        first(other, other, depth, half - 1).wait_send()

    ended = pltpu.make_async_remote_copy(
        src_ref=result.at[0 : n - 1], dst_ref=result.at[0 : n - 1], send_sem=send_two, recv_sem=recv_two,
        device_id={"cell": other}, device_id_type=MESH,
    )
    ended.wait_send()
    ended.wait_recv()
    own.wait()


def shards(wave_energy, courant, sea_mask, lift_weight, back_weight):
    n = lax.axis_size("cell")
    groups, cells = wave_energy.shape
    modes = lift_weight.shape[0]
    depth = -(-groups // 8) * 8
    extra = depth - groups
    if extra:
        wave_energy = jnp.pad(wave_energy, ((0, extra), (0, 0)))
        courant = jnp.pad(courant.reshape(n, groups), ((0, 0), (0, extra))).reshape(-1)
        lift_weight = jnp.pad(
            lift_weight.reshape(modes, n, groups), ((0, 0), (0, 0), (0, extra))
        ).reshape(modes, n * depth)
        back_weight = jnp.pad(
            back_weight.reshape(n, groups, modes), ((0, 0), (0, extra), (0, 0))
        ).reshape(n * depth, modes)
    comps = n * depth
    strips = comps // LANES
    tall = LANES + 2 * EDGE
    buffers = [
        pltpu.VMEM((depth, cells), jnp.float32),
        pltpu.VMEM((strips, LANES), jnp.float32),
        pltpu.VMEM((1, cells), jnp.int32),
        pltpu.VMEM((n, depth + EDGE, LANES), jnp.float32),
        pltpu.VMEM((n, depth + EDGE, LANES), jnp.float32),
        pltpu.VMEM((cells + 2 * EDGE, LANES), jnp.float32),
        pltpu.VMEM((cells + 2 * EDGE, LANES), jnp.float32),
        pltpu.VMEM((strips, LANES + EDGE, LANES), jnp.float32),
        pltpu.VMEM((tall, comps), jnp.bfloat16),
        pltpu.VMEM((tall, modes), jnp.bfloat16),
        pltpu.VMEM((comps, LANES), jnp.float32),
        pltpu.VMEM((n, depth, LANES), jnp.float32),
        pltpu.VMEM((2, strips, EDGE, LANES), jnp.float32),
        pltpu.VMEM((modes, comps), jnp.bfloat16),
        pltpu.VMEM((comps, modes), jnp.bfloat16),
    ]
    held = sum(math.prod(b.shape) * jnp.dtype(b.dtype).itemsize for b in buffers)
    operands = [
        pltpu.with_memory_space_constraint(x, pltpu.HBM)
        for x in (wave_energy, courant.reshape(strips, LANES), sea_mask[None, :], lift_weight, back_weight)
    ]
    out = pl.pallas_call(
        functools.partial(kernel, n),
        out_shape=jax.ShapeDtypeStruct((depth, cells), jnp.float32),
        in_specs=[pl.BlockSpec(memory_space=pltpu.HBM)] * 5,
        out_specs=pl.BlockSpec(memory_space=pl.ANY),
        scratch_shapes=buffers
        + [
            pltpu.SemaphoreType.DMA((5,)),
            pltpu.SemaphoreType.DMA,
            pltpu.SemaphoreType.DMA((2,)),
            pltpu.SemaphoreType.DMA,
            pltpu.SemaphoreType.DMA,
            pltpu.SemaphoreType.DMA,
            pltpu.SemaphoreType.DMA((2,)),
            pltpu.SemaphoreType.DMA((2,)),
        ],
        compiler_params=pltpu.CompilerParams(
            collective_id=0, has_side_effects=True, vmem_limit_bytes=held + 4 * 1024 * 1024
        ),
    )(*operands)
    return out[:groups]


def solution(mesh):
    placed = (P(("member", "cell"), None), P(), P(), P(), P())
    return jax.shard_map(
        shards, mesh=mesh, in_specs=placed, out_specs=P(("member", "cell"), None), check_vma=False
    )
```
